512 devices in a mesh: ctx: 32 (over y_hi, z, core), tp: 16 (over x, y_lo).
Axes of the slice: x: 4, y: 8 (y_hi: 2, y_lo: 4; y = y_hi * 4 + y_lo), z: 8, core: 2. Of those that a mesh axis runs over, the one named last changes fastest.
Arguments:
- features: bfloat16 [4096, 3, 8192], P('ctx', None, 'tp'), may hold values from -6 to 6
- short_filter: float32 [3, 3, 8192], P(None, None, 'tp'), may hold values from -3 to 3
- decay_rate: float32 [16, 8192], P(None, 'tp'), may hold values from 2e-05 to 0.04
- residue: float32 [16, 8192], P(None, 'tp'), may hold values from -2 to 2
- skip: float32 [8192], P('tp'), may hold values from -2 to 2
- out_weight: bfloat16 [8192, 8192], P('tp', 'ctx'), may hold values from -0.125 to 0.125
Outputs:
- mixed: bfloat16 [4096, 8192], P('ctx', 'tp')
The draws below stay inside these ranges and needn't reach their ends.
All inputs are finite; a program needn't handle non-finite values.
Results may differ from the reference program's by a relative error of at most 0.0049.
Values may be sent and summed in bfloat16 or wider, within the bound.
No kernel may reach another device: no remote copies, remote signals or barrier semaphores. Data moves between devices by JAX's collectives and lax.ppermute only.
A program may use at most 64 MiB of HBM per device.

```python
import math
import jax
import jax.numpy as jnp
from jax import lax

D = 8192
MODES = 16
TAPS = 3
TOKENS = 4096
N_TP = 16


def raised(values, key, source, target, parts, factor):
    owner, partner = [(jnp.arange(values.shape[position]) // (values.shape[position] // parts)).reshape([-1 if axis == position else 1 for axis in range(values.ndim)]) for position in (source, target)]
    chosen = jax.random.permutation(key, parts)[partner]
    strong = (owner == chosen) | (owner == (partner + parts // 2) % parts)
    return jnp.where(strong, factor * values, values)


def levels(stream_key, extent, cuts, low, top_value):
    def one(dim, blocks):
        heights = jax.random.uniform(jax.random.fold_in(jax.random.fold_in(stream_key, 6), dim), (blocks,), jnp.float32, low / len(cuts), top_value / len(cuts))
        return jnp.repeat(jnp.exp(heights), extent[dim] // blocks).reshape((-1,) + (1,) * (len(extent) - dim - 1))

    loudness = one(*cuts[0])
    for cut in cuts[1:]:
        loudness = loudness * one(*cut)
    return loudness


def bell_draw(own_key, extent, scale, reach, pieces=(), held_as=jnp.bfloat16):
    loudness = levels(own_key, extent, pieces, -0.22, 0.18) if pieces else 1.0
    values = jax.random.normal(own_key, extent, jnp.float32) * scale * loudness
    return jnp.minimum(jnp.maximum(values, -reach), reach).astype(held_as)


def heavy_noise(key, shape, scale, limit, shards, heavy, kind=jnp.bfloat16):
    array = scale * jax.random.normal(key, shape, jnp.float32)
    if shards:
        array = array * levels(key, shape, shards, -0.22, 0.18)
    return jnp.clip(raised(array, jax.random.fold_in(key, 3), *heavy), -limit, limit).astype(kind)


def setup_inputs(seed: int = 0) -> dict:
    seeds = jax.random.split(jax.random.key(seed), 7)
    return {
        "features": bell_draw(seeds[0], (TOKENS, 3, D), 1.0, 6.0, ((0, 32), (2, 16))),
        "short_filter": bell_draw(seeds[1], (TAPS, 3, D), 0.6, 3.0, ((2, 16),), jnp.float32),
        "decay_rate": jnp.clip(jnp.exp(math.log(0.04) - 7.6009025 * jax.random.uniform(seeds[2], (MODES, D), jnp.float32) ** levels(seeds[2], (MODES, D), ((1, 16),), -0.2, 0.2)), 1.9999999494757503e-05, 0.04),
        "residue": bell_draw(seeds[3], (MODES, D), 0.3, 2.0, ((1, 16),), jnp.float32),
        "skip": bell_draw(seeds[4], (D,), 0.5, 2.0, ((0, 16),), jnp.float32),
        "out_weight": heavy_noise(seeds[5], (D, D), D ** -0.5, 0.125, ((0, 16), (1, 32)), (0, 1, 32, 2.75)),
    }


def reference(features, short_filter, decay_rate, residue, skip, out_weight):
    widened = features.astype(jnp.float32)
    padded = jnp.pad(widened, ((TAPS - 1, 0), (0, 0), (0, 0)))
    filtered = jnp.zeros_like(widened)
    for tap_index in range(TAPS):
        begin = TAPS - 1 - tap_index
        filtered = filtered + short_filter[tap_index][None] * padded[begin:begin + TOKENS]
    query = filtered[:, 0]
    drive = filtered[:, 1] * filtered[:, 2]
    decay = jnp.exp(-decay_rate)
    gain = residue * jnp.sqrt(-jnp.expm1(-2.0 * decay_rate))

    def advance(state, drive_row):
        state = decay * state + drive_row[None]
        return (state, lax.optimization_barrier(jnp.sum(gain * state, axis=0)))
    _, modal = lax.scan(advance, jnp.zeros((MODES, D), jnp.float32), drive)
    response = modal + skip[None] * drive
    gated = (query * response).astype(jnp.bfloat16)
    group_width = D // N_TP

    def add_group(group, total):
        start = (group * group_width).astype(jnp.int32)
        cols = lax.dynamic_slice_in_dim(gated, start, group_width, 1)
        weight_rows = lax.dynamic_slice_in_dim(out_weight, start, group_width, 0)
        return total + jnp.dot(cols, weight_rows, preferred_element_type=jnp.float32)
    total = lax.fori_loop(0, N_TP, add_group, jnp.zeros((TOKENS, D), jnp.float32))
    return total.astype(jnp.bfloat16)
```

```python
import functools

import jax
import jax.numpy as jnp
from jax import lax
from jax.experimental import pallas as pl
from jax.experimental.pallas import tpu as pltpu
from jax.sharding import PartitionSpec as P

AXES = ("ctx", "tp")
EVERY = [
    (yh, z, core, x, yl)
    for yh in range(2)
    for z in range(8)
    for core in range(2)
    for x in range(4)
    for yl in range(4)
]


def flat(yh, z, core, x, yl):
    return ((yh * 8 + z) * 2 + core) * 16 + x * 4 + yl


def move(value, axes, target, sends=lambda *place: True):
    pairs = [(flat(*p), flat(*target(*p))) for p in EVERY if sends(*p)]
    return lax.ppermute(value, axes, pairs)


def from_behind(value, axes, by):
    pairs = [(i, i + by * 16) for i in range(512) if i + by * 16 < 512]
    return lax.ppermute(value, axes, pairs)


VMEM = pl.BlockSpec(memory_space=pltpu.VMEM)
SMEM = pl.BlockSpec(memory_space=pltpu.SMEM)


def spread(ref, value):
    rows = value.shape[0]
    for half in range(2):
        for part in range(4):
            ref[pl.ds(half * 4 + part, rows, stride=8), :] = value[:, part * 128 : part * 128 + 128]


def front_kernel(feat_ref, halo_ref, taps_ref, rate_ref, query_ref, drive_ref, half_ref, end_ref, ext, lam):
    filtered = []
    for f in range(3):
        ext[8:136, :] = feat_ref[f].astype(jnp.float32)
        ext[6:8, :] = halo_ref[f].astype(jnp.float32)
        total = taps_ref[0, f : f + 1, :] * ext[8:136, :]
        total = total + taps_ref[1, f : f + 1, :] * ext[7:135, :]
        filtered.append(total + taps_ref[2, f : f + 1, :] * ext[6:134, :])
    query_ref[...] = filtered[0]
    drive = filtered[1] * filtered[2]
    for half in range(2):
        for part in range(4):
            drive_ref[pl.ds(half * 4 + part, 64, stride=8), :] = drive[
                half * 64 : half * 64 + 64, part * 128 : part * 128 + 128
            ]
    spread(lam, jnp.exp(-rate_ref[...]))
    lams = [lam[m * 8 : m * 8 + 8, :] for m in range(16)]

    def step(t, states):
        now = drive_ref[pl.ds(pl.multiple_of(t * 8, 8), 8), :]
        return tuple(a * s + now for a, s in zip(lams, states))

    states = lax.fori_loop(0, 64, step, tuple(jnp.zeros((8, 128), jnp.float32) for _ in range(16)), unroll=4)
    for m in range(16):
        half_ref[m * 8 : m * 8 + 8, :] = states[m]
    spread(lam, jnp.exp(-64.0 * rate_ref[...]))
    for m in range(16):
        lam[m * 8 : m * 8 + 8, :] = states[m] + pltpu.roll(lam[m * 8 : m * 8 + 8, :] * states[m], 4, 0)
    for part in range(4):
        end_ref[:, part * 128 : part * 128 + 128] = lam[pl.ds(4 + part, 16, stride=8), :]


def back_kernel(query_ref, drive_ref, half_ref, in_ref, rate_ref, gain_ref, skip_ref, out_ref, lam, gain, start, skip, resp):
    spread(start, in_ref[...])
    spread(gain, gain_ref[...])
    spread(lam, jnp.exp(-64.0 * rate_ref[...]))
    first = lax.broadcasted_iota(jnp.int32, (8, 128), 0) < 4
    states = []
    for m in range(16):
        rows = slice(m * 8, m * 8 + 8)
        came = start[rows, :]
        later = lam[rows, :] * came + pltpu.roll(half_ref[rows, :], 4, 0)
        states.append(jnp.where(first, came, later))
    spread(lam, jnp.exp(-rate_ref[...]))
    spread(skip, skip_ref[...])
    lams = [lam[m * 8 : m * 8 + 8, :] for m in range(16)]
    gains = [gain[m * 8 : m * 8 + 8, :] for m in range(16)]
    direct = skip[...]

    def step(t, states):
        rows = pl.ds(pl.multiple_of(t * 8, 8), 8)
        now = drive_ref[rows, :]
        states = tuple(a * s + now for a, s in zip(lams, states))
        sums = [direct * now, None, None, None]
        for m in range(16):
            term = gains[m] * states[m]
            sums[m % 4] = term if sums[m % 4] is None else sums[m % 4] + term
        resp[rows, :] = (sums[0] + sums[1]) + (sums[2] + sums[3])
        return states

    lax.fori_loop(0, 64, step, tuple(states), unroll=2)
    for half in range(2):
        for part in range(4):
            rows, cols = slice(half * 64, half * 64 + 64), slice(part * 128, part * 128 + 128)
            out_ref[rows, cols] = (query_ref[rows, cols] * resp[pl.ds(half * 4 + part, 64, stride=8), :]).astype(jnp.bfloat16)


def mix_kernel(table_ref, *refs):
    s, (fwd, bwd, hf, hb), weights = refs[:4], refs[4:8], refs[8:17]
    keep_ref, send_ref, g, w, acc, g_sem, w_sem = refs[17:]
    own = table_ref[0] == 1
    yl = table_ref[1]
    low = table_ref[2] * 4
    high = table_ref[3] * 4

    def spot(base, j):
        return g.at[base + lax.rem(yl - j + 4, 4)]

    from_own = [(s[j], spot(low, j)) for j in range(4)]
    from_own += [(hf.at[pl.ds(j * 256, 256), :], spot(high, j)) for j in range(2)]
    from_own += [(hb.at[pl.ds(j * 256, 256), :], spot(high, 2 + j)) for j in range(2)]
    from_others = [(fwd.at[pl.ds(j * 256, 256), :], spot(low, j)) for j in range(4)]
    from_others += [(bwd.at[pl.ds(j * 256, 256), :], spot(high, j)) for j in range(4)]

    def channel_copies(pairs):
        return [pltpu.make_async_copy(a, b, g_sem.at[i]) for i, (a, b) in enumerate(pairs)]

    @pl.when(own)
    def _():
        for copy in channel_copies(from_own):
            copy.start()

    @pl.when(jnp.logical_not(own))
    def _():
        for copy in channel_copies(from_others):
            copy.start()

    loads = [pltpu.make_async_copy(weights[i], w.at[i], w_sem.at[i]) for i in range(7)]
    loads += [pltpu.make_async_copy(weights[7 + p], w.at[7, pl.ds(p * 512, 512)], w_sem.at[7 + p]) for p in range(2)]
    for copy in loads:
        copy.start()

    @pl.when(own)
    def _():
        for copy in channel_copies(from_own):
            copy.wait()

    @pl.when(jnp.logical_not(own))
    def _():
        for copy in channel_copies(from_others):
            copy.wait()

    for i in range(8):
        loads[i].wait()
        if i == 7:
            loads[8].wait()
        block = g[table_ref[4 + i]]
        for p in range(2):
            part = jnp.dot(block, w[i, p * 512 : p * 512 + 512, :], preferred_element_type=jnp.float32)
            acc[p] = part if i == 0 else acc[p] + part
    for p in range(2):

        @pl.when(table_ref[12] == p)
        def _():
            for half in range(2):
                cols = slice(half * 256, half * 256 + 256)
                keep_ref[:, cols] = acc[half ^ p, :128, :]
                send_ref[:, cols] = acc[half ^ p, 128:, :]


def front(feat, halo, taps, rate):
    f32 = jnp.float32
    return pl.pallas_call(
        front_kernel,
        out_shape=(
            jax.ShapeDtypeStruct((128, 512), f32),
            jax.ShapeDtypeStruct((512, 128), f32),
            jax.ShapeDtypeStruct((128, 128), f32),
            jax.ShapeDtypeStruct((16, 512), f32),
        ),
        in_specs=[VMEM] * 4,
        out_specs=(VMEM,) * 4,
        scratch_shapes=[pltpu.VMEM((136, 512), f32), pltpu.VMEM((128, 128), f32)],
        cost_estimate=pl.CostEstimate(flops=1, bytes_accessed=1, transcendentals=0),
        name="front",
    )(feat, halo, taps, rate)


def back(query, drive, half, incoming, rate, gain, skip):
    f32 = jnp.float32
    return pl.pallas_call(
        back_kernel,
        out_shape=jax.ShapeDtypeStruct((128, 512), jnp.bfloat16),
        in_specs=[VMEM] * 7,
        out_specs=VMEM,
        scratch_shapes=[pltpu.VMEM((128, 128), f32)] * 3 + [pltpu.VMEM((8, 128), f32), pltpu.VMEM((512, 128), f32)],
        cost_estimate=pl.CostEstimate(flops=1, bytes_accessed=1, transcendentals=0),
        name="back",
    )(query, drive, half, incoming, rate, gain, skip)


def mix(table, *operands):
    out = jax.ShapeDtypeStruct((128, 512), jnp.float32)
    return pl.pallas_call(
        mix_kernel,
        out_shape=(out, out),
        in_specs=[SMEM] + [pl.BlockSpec(memory_space=pl.ANY)] * len(operands),
        out_specs=(VMEM, VMEM),
        scratch_shapes=[
            pltpu.VMEM((8, 256, 512), jnp.bfloat16),
            pltpu.VMEM((8, 1024, 256), jnp.bfloat16),
            pltpu.VMEM((2, 256, 256), jnp.float32),
            pltpu.SemaphoreType.DMA((8,)),
            pltpu.SemaphoreType.DMA((9,)),
        ],
        compiler_params=pltpu.CompilerParams(vmem_limit_bytes=60 * 1024 * 1024),
        cost_estimate=pl.CostEstimate(flops=1_100_000_000, bytes_accessed=7_000_000, transcendentals=0),
        name="mix",
    )(table, *operands)


def body(features, short_filter, decay_rate, residue, skip, out_weight, axes, front, back, mix):
    n_modes, channels = decay_rate.shape
    positions = features.shape[0]
    index = lax.axis_index(axes)
    yl, x, core, z, yh = index % 4, index // 4 % 4, index // 16 % 2, index // 32 % 8, index // 256

    halo = from_behind(features[positions - 2 :], axes, 1)

    def tile(p):
        def target(yh, z, core, x, yl):
            t = yh * 8 + z
            return core ^ p, (x // 2) * 4 + yl, x % 2, t // 4, t % 4

        return target

    weight = jnp.concatenate([move(out_weight, axes, tile(p)) for p in range(2)], axis=0)
    rows = out_weight.shape[0]

    def along(axis, by):
        def target(yh, z, core, x, yl):
            if axis == "z":
                return yh, (z + by) % 8, core, x, yl
            if axis == "x":
                return yh, z, core, (x + by) % 4, yl
            return yh, z, core, x, (yl + by) % 4

        return target

    def other_core(value):
        return move(value, axes, lambda yh, z, core, x, yl: (yh, z, 1 - core, x, yl))

    tie = lax.optimization_barrier
    ups, downs = [weight], [weight]

    def ring():
        ups.append(move(ups[-1], axes, along("z", 1)))
        downs.append(move(downs[-1], axes, along("z", -1)))

    query, drive, half, end = front(features.transpose(1, 0, 2), halo.transpose(1, 0, 2), short_filter, decay_rate)

    incoming = from_behind(end, axes, 1)
    for k in range(5):
        by = 2**k
        if k == 1:
            incoming, ups[0] = tie((incoming, ups[0]))
            downs[0] = ups[0]
            ring()
        incoming = incoming + jnp.exp(-decay_rate * (positions * by)) * from_behind(incoming, axes, by)

    gain = residue * jnp.sqrt(-jnp.expm1(-2.0 * decay_rate))
    incoming, ups[1], downs[1] = tie((incoming, ups[1], downs[1]))
    ring()
    gated = back(query, drive, half, incoming, decay_rate, gain, skip[None])

    both = jnp.concatenate([gated, other_core(gated)], axis=0)

    def mine(yh, z, core, x, yl):
        return x % 2 == core

    def others(yh, z, core, x, yl):
        return x % 2 != core

    near = [both] + [move(both, axes, along("yl", j), mine) for j in range(1, 4)]
    line = jnp.concatenate(near, axis=0)
    line, ups[2], downs[2] = tie((line, ups[2], downs[2]))
    ring()
    fwd = move(line, axes, along("x", 1), mine)
    bwd = move(line, axes, along("x", -1), mine)
    fwd, bwd, ups[3], downs[3] = tie((fwd, bwd, ups[3], downs[3]))
    up_last = move(ups[3][:rows], axes, along("z", 1))
    down_last = move(downs[3][rows:], axes, along("z", -1))
    weights = [ups[0], ups[1], downs[1], ups[2], downs[2], ups[3], downs[3], up_last, down_last]
    half_rows = line.shape[0] // 2
    hf = move(fwd[:half_rows], axes, along("x", 1), others)
    hb = move(bwd[half_rows:], axes, along("x", -1), others)

    own = x % 2 == core
    low = jnp.where(own, x // 2, (x + 3) % 4 // 2)
    high = jnp.where(own, 1 - x // 2, (x + 1) % 4 // 2)
    places = [(z - d) % 8 for d in (0, 1, -1, 2, -2, 3, -3, 4)]
    table = jnp.stack([own.astype(jnp.int32), yl, low, high] + places + [yh]).astype(jnp.int32)
    keep, send = mix(table, *near, fwd, bwd, hf, hb, *weights)
    return (keep + other_core(send)).astype(jnp.bfloat16)


def shards(*arguments):
    return body(*arguments, AXES, front, back, mix)


def solution(mesh):
    in_specs = (
        P("ctx", None, "tp"),
        P(None, None, "tp"),
        P(None, "tp"),
        P(None, "tp"),
        P("tp"),
        P("tp", "ctx"),
    )
    return jax.shard_map(shards, mesh=mesh, in_specs=in_specs, out_specs=P("ctx", "tp"), check_vma=False)
```

```python
import functools

import jax
import jax.numpy as jnp
from jax import lax
from jax.experimental import pallas as pl
from jax.experimental.pallas import tpu as pltpu
from jax.sharding import PartitionSpec as P

AXES = ("ctx", "tp")
EVERY = [
    (yh, z, core, x, yl)
    for yh in range(2)
    for z in range(8)
    for core in range(2)
    for x in range(4)
    for yl in range(4)
]


def flat(yh, z, core, x, yl):
    return ((yh * 8 + z) * 2 + core) * 16 + x * 4 + yl


def move(value, axes, target, sends=lambda *place: True):
    pairs = [(flat(*p), flat(*target(*p))) for p in EVERY if sends(*p)]
    return lax.ppermute(value, axes, pairs)


def from_behind(value, axes, by):
    pairs = [(i, i + by * 16) for i in range(512) if i + by * 16 < 512]
    return lax.ppermute(value, axes, pairs)


VMEM = pl.BlockSpec(memory_space=pltpu.VMEM)
SMEM = pl.BlockSpec(memory_space=pltpu.SMEM)


def spread(ref, value):
    rows = value.shape[0]
    for half in range(2):
        for part in range(4):
            ref[pl.ds(half * 4 + part, rows, stride=8), :] = value[:, part * 128 : part * 128 + 128]


def front_kernel(feat_ref, halo_ref, taps_ref, rate_ref, query_ref, drive_ref, half_ref, end_ref, ext, lam):
    filtered = []
    for f in range(3):
        ext[8:136, :] = feat_ref[f].astype(jnp.float32)
        ext[6:8, :] = halo_ref[f].astype(jnp.float32)
        total = taps_ref[0, f : f + 1, :] * ext[8:136, :]
        total = total + taps_ref[1, f : f + 1, :] * ext[7:135, :]
        filtered.append(total + taps_ref[2, f : f + 1, :] * ext[6:134, :])
    query_ref[...] = filtered[0]
    drive = filtered[1] * filtered[2]
    for half in range(2):
        for part in range(4):
            drive_ref[pl.ds(half * 4 + part, 64, stride=8), :] = drive[
                half * 64 : half * 64 + 64, part * 128 : part * 128 + 128
            ]
    spread(lam, jnp.exp(-rate_ref[...]))
    lams = [lam[m * 8 : m * 8 + 8, :] for m in range(16)]

    def step(t, states):
        now = drive_ref[pl.ds(pl.multiple_of(t * 8, 8), 8), :]
        return tuple(a * s + now for a, s in zip(lams, states))

    states = lax.fori_loop(0, 64, step, tuple(jnp.zeros((8, 128), jnp.float32) for _ in range(16)), unroll=4)
    for m in range(16):
        half_ref[m * 8 : m * 8 + 8, :] = states[m]
    spread(lam, jnp.exp(-64.0 * rate_ref[...]))
    for m in range(16):
        lam[m * 8 : m * 8 + 8, :] = states[m] + pltpu.roll(lam[m * 8 : m * 8 + 8, :] * states[m], 4, 0)
    for part in range(4):
        end_ref[:, part * 128 : part * 128 + 128] = lam[pl.ds(4 + part, 16, stride=8), :]


def back_kernel(query_ref, drive_ref, half_ref, in_ref, rate_ref, gain_ref, skip_ref, out_ref, lam, gain, start, skip, resp):
    spread(start, in_ref[...])
    spread(gain, gain_ref[...])
    spread(lam, jnp.exp(-64.0 * rate_ref[...]))
    first = lax.broadcasted_iota(jnp.int32, (8, 128), 0) < 4
    states = []
    for m in range(16):
        rows = slice(m * 8, m * 8 + 8)
        came = start[rows, :]
        later = lam[rows, :] * came + pltpu.roll(half_ref[rows, :], 4, 0)
        states.append(jnp.where(first, came, later))
    spread(lam, jnp.exp(-rate_ref[...]))
    spread(skip, skip_ref[...])
    lams = [lam[m * 8 : m * 8 + 8, :] for m in range(16)]
    gains = [gain[m * 8 : m * 8 + 8, :] for m in range(16)]
    direct = skip[...]

    def step(t, states):
        rows = pl.ds(pl.multiple_of(t * 8, 8), 8)
        now = drive_ref[rows, :]
        states = tuple(a * s + now for a, s in zip(lams, states))
        sums = [direct * now, None, None, None]
        for m in range(16):
            term = gains[m] * states[m]
            sums[m % 4] = term if sums[m % 4] is None else sums[m % 4] + term
        resp[rows, :] = (sums[0] + sums[1]) + (sums[2] + sums[3])
        return states

    lax.fori_loop(0, 64, step, tuple(states), unroll=2)
    for half in range(2):
        for part in range(4):
            rows, cols = slice(half * 64, half * 64 + 64), slice(part * 128, part * 128 + 128)
            out_ref[rows, cols] = (query_ref[rows, cols] * resp[pl.ds(half * 4 + part, 64, stride=8), :]).astype(jnp.bfloat16)


def mix_kernel(table_ref, *refs):
    line, fwd, bwd, hf, hb = refs[:5]
    weights = refs[5:14]
    keep_ref, send_ref, g, w, acc, g_sem, w_sem = refs[14:]
    own = table_ref[0] == 1
    yl = table_ref[1]
    low, high = table_ref[2], table_ref[3]

    def from_own():
        return [
            pltpu.make_async_copy(line, g.at[low], g_sem.at[0]),
            pltpu.make_async_copy(hf, g.at[high, pl.ds(0, 256)], g_sem.at[1]),
            pltpu.make_async_copy(hb, g.at[high, pl.ds(256, 256)], g_sem.at[2]),
        ]

    def from_others():
        return [
            pltpu.make_async_copy(fwd, g.at[low], g_sem.at[0]),
            pltpu.make_async_copy(bwd, g.at[high], g_sem.at[1]),
        ]

    @pl.when(own)
    def _():
        for copy in from_own():
            copy.start()

    @pl.when(jnp.logical_not(own))
    def _():
        for copy in from_others():
            copy.start()

    loads = [pltpu.make_async_copy(weights[i], w.at[i], w_sem.at[i]) for i in range(7)]
    loads += [pltpu.make_async_copy(weights[7 + p], w.at[7, pl.ds(p * 256, 256)], w_sem.at[7 + p]) for p in range(2)]
    for copy in loads:
        copy.start()
    acc[...] = jnp.zeros_like(acc)

    @pl.when(own)
    def _():
        for copy in from_own():
            copy.wait()

    @pl.when(jnp.logical_not(own))
    def _():
        for copy in from_others():
            copy.wait()

    for i in range(8):
        loads[i].wait()
        if i == 7:
            loads[8].wait()
        place = table_ref[4 + i]
        part = jnp.dot(g[lax.rem(place, 2)], w[i], preferred_element_type=jnp.float32)
        acc[place // 2] += part.reshape(4, 128, 256)
    for d in range(4):
        block = lax.rem(yl + d, 4)
        for half in range(2):
            cols = slice(half * 256, half * 256 + 256)
            keep_ref[d, :, cols] = acc[lax.rem(block, 2) * 2 + half, block // 2 * 2]
            send_ref[d, :, cols] = acc[lax.rem(block, 2) * 2 + half, block // 2 * 2 + 1]


def front(feat, halo, taps, rate):
    f32 = jnp.float32
    return pl.pallas_call(
        front_kernel,
        out_shape=(
            jax.ShapeDtypeStruct((128, 512), f32),
            jax.ShapeDtypeStruct((512, 128), f32),
            jax.ShapeDtypeStruct((128, 128), f32),
            jax.ShapeDtypeStruct((16, 512), f32),
        ),
        in_specs=[VMEM] * 4,
        out_specs=(VMEM,) * 4,
        scratch_shapes=[pltpu.VMEM((136, 512), f32), pltpu.VMEM((128, 128), f32)],
        cost_estimate=pl.CostEstimate(flops=1, bytes_accessed=1, transcendentals=0),
        name="front",
    )(feat, halo, taps, rate)


def back(query, drive, half, incoming, rate, gain, skip):
    f32 = jnp.float32
    return pl.pallas_call(
        back_kernel,
        out_shape=jax.ShapeDtypeStruct((128, 512), jnp.bfloat16),
        in_specs=[VMEM] * 7,
        out_specs=VMEM,
        scratch_shapes=[pltpu.VMEM((128, 128), f32)] * 3 + [pltpu.VMEM((8, 128), f32), pltpu.VMEM((512, 128), f32)],
        cost_estimate=pl.CostEstimate(flops=1, bytes_accessed=1, transcendentals=0),
        name="back",
    )(query, drive, half, incoming, rate, gain, skip)


def mix(table, *operands):
    out = jax.ShapeDtypeStruct((4, 128, 512), jnp.float32)
    return pl.pallas_call(
        mix_kernel,
        out_shape=(out, out),
        in_specs=[SMEM] + [pl.BlockSpec(memory_space=pl.ANY)] * len(operands),
        out_specs=(VMEM, VMEM),
        scratch_shapes=[
            pltpu.VMEM((2, 512, 512), jnp.bfloat16),
            pltpu.VMEM((8, 512, 256), jnp.bfloat16),
            pltpu.VMEM((4, 4, 128, 256), jnp.float32),
            pltpu.SemaphoreType.DMA((3,)),
            pltpu.SemaphoreType.DMA((9,)),
        ],
        compiler_params=pltpu.CompilerParams(vmem_limit_bytes=60 * 1024 * 1024),
        cost_estimate=pl.CostEstimate(flops=1_100_000_000, bytes_accessed=7_000_000, transcendentals=0),
        name="mix",
    )(table, *operands)


def body(features, short_filter, decay_rate, residue, skip, out_weight, axes, front, back, mix):
    n_modes, channels = decay_rate.shape
    positions = features.shape[0]
    index = lax.axis_index(axes)
    yl, x, core, z = index % 4, index // 4 % 4, index // 16 % 2, index // 32 % 8

    halo = from_behind(features[positions - 2 :], axes, 1)

    tie = lax.optimization_barrier
    rows = out_weight.shape[0]

    def place(yh, z, core, x, yl):
        return yh, z // 4 * 4 + core * 2 + x // 2, x % 2, z % 4, yl

    def along(axis, by):
        def target(yh, z, core, x, yl):
            if axis == "z":
                return yh, (z + by) % 8, core, x, yl
            if axis == "x":
                return yh, z, core, (x + by) % 4, yl
            return yh, z, core, x, (yl + by) % 4

        return target

    def mine(yh, z, core, x, yl):
        return x % 2 == core

    def others(yh, z, core, x, yl):
        return x % 2 != core

    def other_core(value, sends=lambda *place: True):
        return move(value, axes, lambda yh, z, core, x, yl: (yh, z, 1 - core, x, yl), sends)

    weight = move(out_weight, axes, place)
    ups, downs = [weight], [weight]

    def ring():
        ups.append(move(ups[-1], axes, along("z", 1)))
        downs.append(move(downs[-1], axes, along("z", -1)))

    query, drive, half, end = front(features.transpose(1, 0, 2), halo.transpose(1, 0, 2), short_filter, decay_rate)
    end, weight = tie((end, weight))

    incoming = from_behind(end, axes, 1)
    for k in range(5):
        by = 2**k
        incoming = incoming + jnp.exp(-decay_rate * (positions * by)) * from_behind(incoming, axes, by)

    gain = residue * jnp.sqrt(-jnp.expm1(-2.0 * decay_rate))
    incoming, weight = tie((incoming, weight))
    ups[0] = downs[0] = weight
    ring()
    gated = back(query, drive, half, incoming, decay_rate, gain, skip[None])

    both = jnp.concatenate([gated, other_core(gated, others)], axis=0)
    both, ups[1], downs[1] = tie((both, ups[1], downs[1]))
    ring()
    beyond = move(both, axes, lambda yh, z, core, x, yl: (1 - yh, z, core, x, yl), mine)
    line = jnp.concatenate([both, beyond], axis=0)
    line, ups[2], downs[2] = tie((line, ups[2], downs[2]))
    ring()
    fwd = move(line, axes, along("x", 1), mine)
    bwd = move(line, axes, along("x", -1), mine)
    fwd, bwd, ups[3], downs[3] = tie((fwd, bwd, ups[3], downs[3]))
    up_last = move(ups[3][: rows // 2], axes, along("z", 1))
    down_last = move(downs[3][rows // 2 :], axes, along("z", -1))
    weights = [ups[0], ups[1], downs[1], ups[2], downs[2], ups[3], downs[3], up_last, down_last]
    half_rows = line.shape[0] // 2
    hf = move(fwd[:half_rows], axes, along("x", 1), others)
    hb = move(bwd[half_rows:], axes, along("x", -1), others)

    own = x % 2 == core
    low = jnp.where(own, x // 2, (x + 3) % 4 // 2)
    high = jnp.where(own, 1 - x // 2, (x + 1) % 4 // 2)
    places = [(z - d) % 8 for d in (0, 1, -1, 2, -2, 3, -3, 4)]
    table = jnp.stack([own.astype(jnp.int32), yl, low, high] + places).astype(jnp.int32)
    keep, send = mix(table, line, fwd, bwd, hf, hb, *weights)

    blocks = keep + other_core(send)
    parts = [move(blocks[d].astype(jnp.bfloat16), axes, along("yl", d)) for d in range(1, 4)]
    total = blocks[0] + sum(part.astype(jnp.float32) for part in parts)
    return move(
        total.astype(jnp.bfloat16), axes, lambda yh, z, core, x, yl: (yh ^ (yl // 2), z, core, yh * 2 + yl % 2, x)
    )


def shards(*arguments):
    return body(*arguments, AXES, front, back, mix)


def solution(mesh):
    in_specs = (
        P("ctx", None, "tp"),
        P(None, None, "tp"),
        P(None, "tp"),
        P(None, "tp"),
        P("tp"),
        P("tp", "ctx"),
    )
    return jax.shard_map(shards, mesh=mesh, in_specs=in_specs, out_specs=P("ctx", "tp"), check_vma=False)
```

```python
import functools

import jax
import jax.numpy as jnp
from jax import lax
from jax.experimental import pallas as pl
from jax.experimental.pallas import tpu as pltpu
from jax.sharding import PartitionSpec as P

AXES = ("ctx", "tp")
EVERY = [
    (yh, z, core, x, yl)
    for yh in range(2)
    for z in range(8)
    for core in range(2)
    for x in range(4)
    for yl in range(4)
]


def flat(yh, z, core, x, yl):
    return ((yh * 8 + z) * 2 + core) * 16 + x * 4 + yl


def move(value, axes, target, sends=lambda *place: True):
    pairs = [(flat(*p), flat(*target(*p))) for p in EVERY if sends(*p)]
    return lax.ppermute(value, axes, pairs)


def from_behind(value, axes, by):
    pairs = [(i, i + by * 16) for i in range(512) if i + by * 16 < 512]
    return lax.ppermute(value, axes, pairs)


VMEM = pl.BlockSpec(memory_space=pltpu.VMEM)
SMEM = pl.BlockSpec(memory_space=pltpu.SMEM)


def spread(ref, value):
    rows = value.shape[0]
    for half in range(2):
        for part in range(4):
            ref[pl.ds(half * 4 + part, rows, stride=8), :] = value[:, part * 128 : part * 128 + 128]


def first_kernel(feat_ref, taps_ref, rate_ref, out_ref, ext, drive_ref, lam):
    both = []
    sides = []
    for f in (1, 2):
        taps = [taps_ref[j, f : f + 1, :] for j in range(3)]
        ext[8:136, :] = feat_ref[f].astype(jnp.float32)
        ext[0:8, :] = jnp.zeros((8, 512), jnp.float32)
        total = taps[0] * ext[8:136, :] + taps[1] * ext[7:135, :] + taps[2] * ext[6:134, :]
        both.append(total)
        last = ext[135:136, :]
        sides.append((total[0:1], total[1:2], taps[1] * last + taps[2] * ext[134:135, :], taps[2] * last))
    drive = both[0] * both[1]
    side = jnp.concatenate([sides[0][0], sides[1][0], sides[0][1], sides[1][1], sides[0][2], sides[1][2], sides[0][3], sides[1][3]], axis=0)
    pack_positions(drive_ref, drive)
    spread(lam, jnp.exp(-rate_ref[...]))
    lams = [lam[m * 8 : m * 8 + 8, :] for m in range(16)]

    def step(t, states):
        now = drive_ref[pl.ds(pl.multiple_of(t * 8, 8), 8), :]
        return tuple(a * s + now for a, s in zip(lams, states))

    states = lax.fori_loop(0, 64, step, tuple(jnp.zeros((8, 128), jnp.float32) for _ in range(16)), unroll=4)
    spread(lam, jnp.exp(-64.0 * rate_ref[...]))
    for part in range(4):
        for pair in range(8):
            out_ref[pair * 4 + part, 8:16, :] = side[:, part * 128 : part * 128 + 128]
    for m in range(16):
        end = states[m] + pltpu.roll(lam[m * 8 : m * 8 + 8, :] * states[m], 4, 0)
        for part in range(4):
            out_ref[m // 2 * 4 + part, m % 2 : m % 2 + 1, :] = end[4 + part : 5 + part]


def carry_kernel(ends_ref, rate_ref, out_ref):
    rate = rate_ref[...]
    whole, late, later = jnp.exp(-128.0 * rate), jnp.exp(-127.0 * rate), jnp.exp(-126.0 * rate)
    state = jnp.zeros((2, 128), jnp.float32)
    for k in range(32):
        out_ref[k] = state
        end = ends_ref[k, 0:2, :]
        if k > 0:
            here, before = ends_ref[k, 8:12, :], ends_ref[k - 1, 12:16, :]
            full = here + before
            end = end + late * (full[0:1] * full[1:2] - here[0:1] * here[1:2])
            end = end + later * (full[2:3] * full[3:4] - here[2:3] * here[3:4])
        state = whole * state + end


def pack_positions(ref, drive):
    for half in range(2):
        for part in range(4):
            ref[pl.ds(half * 4 + part, 64, stride=8), :] = drive[
                half * 64 : half * 64 + 64, part * 128 : part * 128 + 128
            ]


def middle_kernel(feat_ref, halo_ref, taps_ref, rate_ref, query_ref, drive_ref, half_ref, ext, lam):
    filtered = []
    for f in range(3):
        ext[8:136, :] = feat_ref[f].astype(jnp.float32)
        ext[6:8, :] = halo_ref[f].astype(jnp.float32)
        total = taps_ref[0, f : f + 1, :] * ext[8:136, :]
        total = total + taps_ref[1, f : f + 1, :] * ext[7:135, :]
        filtered.append(total + taps_ref[2, f : f + 1, :] * ext[6:134, :])
    query_ref[...] = filtered[0]
    pack_positions(drive_ref, filtered[1] * filtered[2])
    spread(lam, jnp.exp(-rate_ref[...]))
    lams = [lam[m * 8 : m * 8 + 8, :] for m in range(16)]

    def step(t, states):
        now = drive_ref[pl.ds(pl.multiple_of(t * 8, 8), 8), :]
        return tuple(a * s + now for a, s in zip(lams, states))

    states = lax.fori_loop(0, 64, step, tuple(jnp.zeros((8, 128), jnp.float32) for _ in range(16)), unroll=4)
    for m in range(16):
        half_ref[m * 8 : m * 8 + 8, :] = states[m]


def back_kernel(query_ref, drive_ref, half_ref, in_ref, rate_ref, gain_ref, skip_ref, out_ref, lam, gain, skip, resp):
    spread(gain, gain_ref[...])
    spread(lam, jnp.exp(-64.0 * rate_ref[...]))
    states = []
    for m in range(16):
        rows = slice(m * 8, m * 8 + 8)
        came = in_ref[pl.ds(m // 2 * 8 + m % 2, 4, stride=2), :]
        later = lam[m * 8 : m * 8 + 4, :] * came + half_ref[m * 8 : m * 8 + 4, :]
        states.append(jnp.concatenate([came, later], axis=0))
    spread(lam, jnp.exp(-rate_ref[...]))
    spread(skip, skip_ref[...])
    lams = [lam[m * 8 : m * 8 + 8, :] for m in range(16)]
    gains = [gain[m * 8 : m * 8 + 8, :] for m in range(16)]
    direct = skip[...]

    def step(t, states):
        rows = pl.ds(pl.multiple_of(t * 8, 8), 8)
        now = drive_ref[rows, :]
        states = tuple(a * s + now for a, s in zip(lams, states))
        sums = [direct * now, None, None, None]
        for m in range(16):
            term = gains[m] * states[m]
            sums[m % 4] = term if sums[m % 4] is None else sums[m % 4] + term
        resp[rows, :] = (sums[0] + sums[1]) + (sums[2] + sums[3])
        return states

    lax.fori_loop(0, 64, step, tuple(states), unroll=2)
    for half in range(2):
        for part in range(4):
            rows, cols = slice(half * 64, half * 64 + 64), slice(part * 128, part * 128 + 128)
            out_ref[rows, cols] = (query_ref[rows, cols] * resp[pl.ds(half * 4 + part, 64, stride=8), :]).astype(jnp.bfloat16)


def mix_kernel(table_ref, *refs):
    line, fwd, bwd, hf, hb, weights = refs[:6]
    keep_ref, send_ref, g, w, acc, g_sem, w_sem = refs[6:]
    own = table_ref[0] == 1
    yl = table_ref[1]
    low, high = table_ref[2], table_ref[3]

    def from_own():
        return [
            pltpu.make_async_copy(line, g.at[low], g_sem.at[0]),
            pltpu.make_async_copy(hf, g.at[high, pl.ds(0, 256)], g_sem.at[1]),
            pltpu.make_async_copy(hb, g.at[high, pl.ds(256, 256)], g_sem.at[2]),
        ]

    def from_others():
        return [
            pltpu.make_async_copy(fwd, g.at[low], g_sem.at[0]),
            pltpu.make_async_copy(bwd, g.at[high], g_sem.at[1]),
        ]

    @pl.when(own)
    def _():
        for copy in from_own():
            copy.start()

    @pl.when(jnp.logical_not(own))
    def _():
        for copy in from_others():
            copy.start()

    loads = [pltpu.make_async_copy(weights.at[i], w.at[i], w_sem.at[i]) for i in range(8)]
    for copy in loads:
        copy.start()

    @pl.when(own)
    def _():
        for copy in from_own():
            copy.wait()

    @pl.when(jnp.logical_not(own))
    def _():
        for copy in from_others():
            copy.wait()

    for i in range(8):
        loads[i].wait()
        part = jnp.dot(g[i % 2], w[i], preferred_element_type=jnp.float32).reshape(4, 128, 256)
        acc[i // 2] = part if i % 2 == 0 else acc[i // 2] + part
    for d in range(4):
        block = lax.rem(yl + d, 4)
        for half in range(2):
            cols = slice(half * 256, half * 256 + 256)
            keep_ref[d, :, cols] = acc[lax.rem(block, 2) * 2 + half, block // 2 * 2]
            send_ref[d, :, cols] = acc[lax.rem(block, 2) * 2 + half, block // 2 * 2 + 1]


TINY = pl.CostEstimate(flops=1, bytes_accessed=1, transcendentals=0)
F32 = jnp.float32


def first(feat, taps, rate):
    return pl.pallas_call(
        first_kernel,
        out_shape=jax.ShapeDtypeStruct((32, 16, 128), F32),
        in_specs=[VMEM] * 3,
        out_specs=VMEM,
        scratch_shapes=[pltpu.VMEM((136, 512), F32), pltpu.VMEM((512, 128), F32), pltpu.VMEM((128, 128), F32)],
        cost_estimate=TINY,
        name="first",
    )(feat, taps, rate)


def carry(ends, rate):
    return pl.pallas_call(
        carry_kernel,
        out_shape=jax.ShapeDtypeStruct((32, 2, 128), F32),
        in_specs=[VMEM] * 2,
        out_specs=VMEM,
        cost_estimate=TINY,
        name="carry",
    )(ends, rate)


def middle(feat, halo, taps, rate):
    return pl.pallas_call(
        middle_kernel,
        out_shape=(
            jax.ShapeDtypeStruct((128, 512), F32),
            jax.ShapeDtypeStruct((512, 128), F32),
            jax.ShapeDtypeStruct((128, 128), F32),
        ),
        in_specs=[VMEM] * 4,
        out_specs=(VMEM,) * 3,
        scratch_shapes=[pltpu.VMEM((136, 512), F32), pltpu.VMEM((128, 128), F32)],
        cost_estimate=TINY,
        name="middle",
    )(feat, halo, taps, rate)


def back(query, drive, half, incoming, rate, gain, skip):
    return pl.pallas_call(
        back_kernel,
        out_shape=jax.ShapeDtypeStruct((128, 512), jnp.bfloat16),
        in_specs=[VMEM] * 7,
        out_specs=VMEM,
        scratch_shapes=[pltpu.VMEM((128, 128), F32)] * 2 + [pltpu.VMEM((8, 128), F32), pltpu.VMEM((512, 128), F32)],
        cost_estimate=TINY,
        name="back",
    )(query, drive, half, incoming, rate, gain, skip)


def mix(table, *operands):
    out = jax.ShapeDtypeStruct((4, 128, 512), jnp.float32)
    return pl.pallas_call(
        mix_kernel,
        out_shape=(out, out),
        in_specs=[SMEM] + [pl.BlockSpec(memory_space=pl.ANY)] * len(operands),
        out_specs=(VMEM, VMEM),
        scratch_shapes=[
            pltpu.VMEM((2, 512, 512), jnp.bfloat16),
            pltpu.VMEM((8, 512, 256), jnp.bfloat16),
            pltpu.VMEM((4, 4, 128, 256), jnp.float32),
            pltpu.SemaphoreType.DMA((3,)),
            pltpu.SemaphoreType.DMA((8,)),
        ],
        compiler_params=pltpu.CompilerParams(vmem_limit_bytes=60 * 1024 * 1024),
        cost_estimate=pl.CostEstimate(flops=1_100_000_000, bytes_accessed=7_000_000, transcendentals=0),
        name="mix",
    )(table, *operands)


def body(features, short_filter, decay_rate, residue, skip, out_weight, axes, first, carry, middle, back, mix):
    positions = features.shape[0]
    index = lax.axis_index(axes)
    yl, x, core = index % 4, index // 4 % 4, index // 16 % 2

    halo = from_behind(features[positions - 2 :], axes, 1)

    tie = lax.optimization_barrier
    def place(yh, z, core, x, yl):
        return yh, z // 4 * 4 + core * 2 + x // 2, x % 2, z % 4, yl

    def along(axis, by):
        def target(yh, z, core, x, yl):
            if axis == "z":
                return yh, (z + by) % 8, core, x, yl
            if axis == "x":
                return yh, z, core, (x + by) % 4, yl
            return yh, z, core, x, (yl + by) % 4

        return target

    def mine(yh, z, core, x, yl):
        return x % 2 == core

    def others(yh, z, core, x, yl):
        return x % 2 != core

    def other_core(value, sends=lambda *place: True):
        return move(value, axes, lambda yh, z, core, x, yl: (yh, z, 1 - core, x, yl), sends)

    weight = move(out_weight, axes, place)
    along_z = [[(yh * 8 + z) * 2 + core for z in range(8)] for yh in range(2) for core in range(2)]

    feat = features.transpose(1, 0, 2)
    ends = first(feat, short_filter, decay_rate)
    ends, weight = tie((ends, weight))
    weights = lax.all_gather(weight, "ctx", axis_index_groups=along_z)
    ends = lax.all_to_all(ends, "ctx", 0, 0, tiled=True)
    ctx = index // 16
    rate = lax.dynamic_slice(decay_rate, (ctx // 4 * 2, ctx % 4 * 128), (2, 128))
    incoming = lax.all_to_all(carry(ends, rate), "ctx", 0, 0, tiled=True).reshape(64, 128)

    query, drive, half = middle(feat, halo.transpose(1, 0, 2), short_filter, decay_rate)
    gain = residue * jnp.sqrt(-jnp.expm1(-2.0 * decay_rate))
    gated = back(query, drive, half, incoming, decay_rate, gain, skip[None])

    both = jnp.concatenate([gated, other_core(gated, others)], axis=0)
    beyond = move(both, axes, lambda yh, z, core, x, yl: (1 - yh, z, core, x, yl), mine)
    line = jnp.concatenate([both, beyond], axis=0)
    fwd = move(line, axes, along("x", 1), mine)
    bwd = move(line, axes, along("x", -1), mine)
    half_rows = line.shape[0] // 2
    hf = move(fwd[:half_rows], axes, along("x", 1), others)
    hb = move(bwd[half_rows:], axes, along("x", -1), others)

    own = x % 2 == core
    low = jnp.where(own, x // 2, (x + 3) % 4 // 2)
    high = jnp.where(own, 1 - x // 2, (x + 1) % 4 // 2)
    table = jnp.stack([own.astype(jnp.int32), yl, low, high]).astype(jnp.int32)
    keep, send = mix(table, line, fwd, bwd, hf, hb, weights)

    blocks = keep + other_core(send)
    parts = [move(blocks[d].astype(jnp.bfloat16), axes, along("yl", d)) for d in range(1, 4)]
    total = blocks[0] + sum(part.astype(jnp.float32) for part in parts)
    return move(
        total.astype(jnp.bfloat16), axes, lambda yh, z, core, x, yl: (yh ^ (yl // 2), z, core, yh * 2 + yl % 2, x)
    )


def shards(*arguments):
    return body(*arguments, AXES, first, carry, middle, back, mix)


def solution(mesh):
    in_specs = (
        P("ctx", None, "tp"),
        P(None, None, "tp"),
        P(None, "tp"),
        P(None, "tp"),
        P("tp"),
        P("tp", "ctx"),
    )
    return jax.shard_map(shards, mesh=mesh, in_specs=in_specs, out_specs=P("ctx", "tp"), check_vma=False)
```

```python
import functools

import jax
import jax.numpy as jnp
from jax import lax
from jax.experimental import pallas as pl
from jax.experimental.pallas import tpu as pltpu
from jax.sharding import PartitionSpec as P

AXES = ("ctx", "tp")
EVERY = [
    (yh, z, core, x, yl)
    for yh in range(2)
    for z in range(8)
    for core in range(2)
    for x in range(4)
    for yl in range(4)
]


def flat(yh, z, core, x, yl):
    return ((yh * 8 + z) * 2 + core) * 16 + x * 4 + yl


def move(value, axes, target, sends=lambda *place: True):
    pairs = [(flat(*p), flat(*target(*p))) for p in EVERY if sends(*p)]
    return lax.ppermute(value, axes, pairs)


def from_behind(value, axes, by):
    pairs = [(i, i + by * 16) for i in range(512) if i + by * 16 < 512]
    return lax.ppermute(value, axes, pairs)


VMEM = pl.BlockSpec(memory_space=pltpu.VMEM)
SMEM = pl.BlockSpec(memory_space=pltpu.SMEM)


def spread(ref, value):
    rows = value.shape[0]
    for half in range(2):
        for part in range(4):
            ref[pl.ds(half * 4 + part, rows, stride=8), :] = value[:, part * 128 : part * 128 + 128]


def first_kernel(feat_ref, taps_ref, rate_ref, out_ref, ext, drive_ref, lam):
    both = []
    sides = []
    for f in (1, 2):
        taps = [taps_ref[j, f : f + 1, :] for j in range(3)]
        ext[8:136, :] = feat_ref[f].astype(jnp.float32)
        ext[0:8, :] = jnp.zeros((8, 512), jnp.float32)
        total = taps[0] * ext[8:136, :] + taps[1] * ext[7:135, :] + taps[2] * ext[6:134, :]
        both.append(total)
        last = ext[135:136, :]
        sides.append((total[0:1], total[1:2], taps[1] * last + taps[2] * ext[134:135, :], taps[2] * last))
    drive = both[0] * both[1]
    side = jnp.concatenate([sides[0][0], sides[1][0], sides[0][1], sides[1][1], sides[0][2], sides[1][2], sides[0][3], sides[1][3]], axis=0)
    pack_positions(drive_ref, drive)
    spread(lam, jnp.exp(-rate_ref[...]))
    lams = [lam[m * 8 : m * 8 + 8, :] for m in range(16)]

    def step(t, states):
        now = drive_ref[pl.ds(pl.multiple_of(t * 8, 8), 8), :]
        return tuple(a * s + now for a, s in zip(lams, states))

    states = lax.fori_loop(0, 64, step, tuple(jnp.zeros((8, 128), jnp.float32) for _ in range(16)), unroll=4)
    spread(lam, jnp.exp(-64.0 * rate_ref[...]))
    for part in range(4):
        for pair in range(8):
            out_ref[pair * 4 + part, 8:16, :] = side[:, part * 128 : part * 128 + 128]
    for m in range(16):
        end = states[m] + pltpu.roll(lam[m * 8 : m * 8 + 8, :] * states[m], 4, 0)
        for part in range(4):
            out_ref[m // 2 * 4 + part, m % 2 : m % 2 + 1, :] = end[4 + part : 5 + part]


def carry_kernel(ends_ref, rate_ref, out_ref):
    rate = rate_ref[...]
    whole, late, later = jnp.exp(-128.0 * rate), jnp.exp(-127.0 * rate), jnp.exp(-126.0 * rate)
    state = jnp.zeros((2, 128), jnp.float32)
    for k in range(32):
        out_ref[k] = state
        end = ends_ref[k, 0:2, :]
        if k > 0:
            here, before = ends_ref[k, 8:12, :], ends_ref[k - 1, 12:16, :]
            full = here + before
            end = end + late * (full[0:1] * full[1:2] - here[0:1] * here[1:2])
            end = end + later * (full[2:3] * full[3:4] - here[2:3] * here[3:4])
        state = whole * state + end


def pack_positions(ref, drive):
    for half in range(2):
        for part in range(4):
            ref[pl.ds(half * 4 + part, 64, stride=8), :] = drive[
                half * 64 : half * 64 + 64, part * 128 : part * 128 + 128
            ]


def middle_kernel(feat_ref, halo_ref, taps_ref, rate_ref, query_ref, drive_ref, half_ref, ext, lam):
    filtered = []
    for f in range(3):
        ext[8:136, :] = feat_ref[f].astype(jnp.float32)
        ext[6:8, :] = halo_ref[f].astype(jnp.float32)
        total = taps_ref[0, f : f + 1, :] * ext[8:136, :]
        total = total + taps_ref[1, f : f + 1, :] * ext[7:135, :]
        filtered.append(total + taps_ref[2, f : f + 1, :] * ext[6:134, :])
    query_ref[...] = filtered[0]
    pack_positions(drive_ref, filtered[1] * filtered[2])
    spread(lam, jnp.exp(-rate_ref[...]))
    lams = [lam[m * 8 : m * 8 + 8, :] for m in range(16)]

    def step(t, states):
        now = drive_ref[pl.ds(pl.multiple_of(t * 8, 8), 8), :]
        return tuple(a * s + now for a, s in zip(lams, states))

    states = lax.fori_loop(0, 64, step, tuple(jnp.zeros((8, 128), jnp.float32) for _ in range(16)), unroll=4)
    for m in range(16):
        half_ref[m * 8 : m * 8 + 8, :] = states[m]


def back_kernel(query_ref, drive_ref, half_ref, in_ref, rate_ref, gain_ref, skip_ref, out_ref, lam, gain, skip, resp):
    spread(gain, gain_ref[...])
    spread(lam, jnp.exp(-64.0 * rate_ref[...]))
    states = []
    for m in range(16):
        rows = slice(m * 8, m * 8 + 8)
        came = in_ref[pl.ds(m // 2 * 8 + m % 2, 4, stride=2), :]
        later = lam[m * 8 : m * 8 + 4, :] * came + half_ref[m * 8 : m * 8 + 4, :]
        states.append(jnp.concatenate([came, later], axis=0))
    spread(lam, jnp.exp(-rate_ref[...]))
    spread(skip, skip_ref[...])
    lams = [lam[m * 8 : m * 8 + 8, :] for m in range(16)]
    gains = [gain[m * 8 : m * 8 + 8, :] for m in range(16)]
    direct = skip[...]

    def step(t, states):
        rows = pl.ds(pl.multiple_of(t * 8, 8), 8)
        now = drive_ref[rows, :]
        states = tuple(a * s + now for a, s in zip(lams, states))
        sums = [direct * now, None, None, None]
        for m in range(16):
            term = gains[m] * states[m]
            sums[m % 4] = term if sums[m % 4] is None else sums[m % 4] + term
        resp[rows, :] = (sums[0] + sums[1]) + (sums[2] + sums[3])
        return states

    lax.fori_loop(0, 64, step, tuple(states), unroll=2)
    for half in range(2):
        for part in range(4):
            rows, cols = slice(half * 64, half * 64 + 64), slice(part * 128, part * 128 + 128)
            out_ref[rows, cols] = (query_ref[rows, cols] * resp[pl.ds(half * 4 + part, 64, stride=8), :]).astype(jnp.bfloat16)


def mix_kernel(table_ref, *refs):
    line, fwd, bwd, hf, hb, weights = refs[:6]
    keep_ref, send_ref, g, w, g_sem, w_sem = refs[6:]
    own = table_ref[0] == 1
    yl = table_ref[1]
    low, high = table_ref[2], table_ref[3]

    def from_own():
        return [
            pltpu.make_async_copy(line, g.at[low], g_sem.at[0]),
            pltpu.make_async_copy(hf, g.at[high, pl.ds(0, 256)], g_sem.at[1]),
            pltpu.make_async_copy(hb, g.at[high, pl.ds(256, 256)], g_sem.at[2]),
        ]

    def from_others():
        return [
            pltpu.make_async_copy(fwd, g.at[low], g_sem.at[0]),
            pltpu.make_async_copy(bwd, g.at[high], g_sem.at[1]),
        ]

    @pl.when(own)
    def _():
        for copy in from_own():
            copy.start()

    @pl.when(jnp.logical_not(own))
    def _():
        for copy in from_others():
            copy.start()

    loads = [pltpu.make_async_copy(weights.at[i], w.at[i], w_sem.at[i]) for i in range(8)]
    for copy in loads:
        copy.start()

    @pl.when(own)
    def _():
        for copy in from_own():
            copy.wait()

    @pl.when(jnp.logical_not(own))
    def _():
        for copy in from_others():
            copy.wait()

    for i in range(4):
        loads[2 * i].wait()
        loads[2 * i + 1].wait()
        part = jnp.dot(g[0], w[2 * i], preferred_element_type=jnp.float32)
        part = part + jnp.dot(g[1], w[2 * i + 1], preferred_element_type=jnp.float32)
        cols = slice(i % 2 * 256, i % 2 * 256 + 256)
        for far in range(2):
            d = lax.rem(far * 2 + i // 2 - yl + 4, 4)
            keep_ref[d, :, cols] = part[far * 256 : far * 256 + 128]
            send_ref[d, :, cols] = part[far * 256 + 128 : far * 256 + 256]


TINY = pl.CostEstimate(flops=1, bytes_accessed=1, transcendentals=0)
F32 = jnp.float32


def first(feat, taps, rate):
    return pl.pallas_call(
        first_kernel,
        out_shape=jax.ShapeDtypeStruct((32, 16, 128), F32),
        in_specs=[VMEM] * 3,
        out_specs=VMEM,
        scratch_shapes=[pltpu.VMEM((136, 512), F32), pltpu.VMEM((512, 128), F32), pltpu.VMEM((128, 128), F32)],
        cost_estimate=TINY,
        name="first",
    )(feat, taps, rate)


def carry(ends, rate):
    return pl.pallas_call(
        carry_kernel,
        out_shape=jax.ShapeDtypeStruct((32, 2, 128), F32),
        in_specs=[VMEM] * 2,
        out_specs=VMEM,
        cost_estimate=TINY,
        name="carry",
    )(ends, rate)


def middle(feat, halo, taps, rate):
    return pl.pallas_call(
        middle_kernel,
        out_shape=(
            jax.ShapeDtypeStruct((128, 512), F32),
            jax.ShapeDtypeStruct((512, 128), F32),
            jax.ShapeDtypeStruct((128, 128), F32),
        ),
        in_specs=[VMEM] * 4,
        out_specs=(VMEM,) * 3,
        scratch_shapes=[pltpu.VMEM((136, 512), F32), pltpu.VMEM((128, 128), F32)],
        cost_estimate=TINY,
        name="middle",
    )(feat, halo, taps, rate)


def back(query, drive, half, incoming, rate, gain, skip):
    return pl.pallas_call(
        back_kernel,
        out_shape=jax.ShapeDtypeStruct((128, 512), jnp.bfloat16),
        in_specs=[VMEM] * 7,
        out_specs=VMEM,
        scratch_shapes=[pltpu.VMEM((128, 128), F32)] * 2 + [pltpu.VMEM((8, 128), F32), pltpu.VMEM((512, 128), F32)],
        cost_estimate=TINY,
        name="back",
    )(query, drive, half, incoming, rate, gain, skip)


def mix(table, *operands):
    out = jax.ShapeDtypeStruct((4, 128, 512), jnp.float32)
    return pl.pallas_call(
        mix_kernel,
        out_shape=(out, out),
        in_specs=[SMEM] + [pl.BlockSpec(memory_space=pl.ANY)] * len(operands),
        out_specs=(VMEM, VMEM),
        scratch_shapes=[
            pltpu.VMEM((2, 512, 512), jnp.bfloat16),
            pltpu.VMEM((8, 512, 256), jnp.bfloat16),
            pltpu.SemaphoreType.DMA((3,)),
            pltpu.SemaphoreType.DMA((8,)),
        ],
        compiler_params=pltpu.CompilerParams(vmem_limit_bytes=60 * 1024 * 1024),
        cost_estimate=pl.CostEstimate(flops=1_100_000_000, bytes_accessed=7_000_000, transcendentals=0),
        name="mix",
    )(table, *operands)


def body(features, short_filter, decay_rate, residue, skip, out_weight, axes, first, carry, middle, back, mix):
    positions = features.shape[0]
    index = lax.axis_index(axes)
    yl, x, core = index % 4, index // 4 % 4, index // 16 % 2

    halo = from_behind(features[positions - 2 :], axes, 1)

    tie = lax.optimization_barrier
    def place(yh, z, core, x, yl):
        return yh, z // 4 * 4 + core * 2 + x // 2, x % 2, z % 4, yl

    def along(axis, by):
        def target(yh, z, core, x, yl):
            if axis == "z":
                return yh, (z + by) % 8, core, x, yl
            if axis == "x":
                return yh, z, core, (x + by) % 4, yl
            return yh, z, core, x, (yl + by) % 4

        return target

    def mine(yh, z, core, x, yl):
        return x % 2 == core

    def others(yh, z, core, x, yl):
        return x % 2 != core

    def other_core(value, sends=lambda *place: True):
        return move(value, axes, lambda yh, z, core, x, yl: (yh, z, 1 - core, x, yl), sends)

    weight = move(out_weight, axes, place)
    along_z = [[(yh * 8 + z) * 2 + core for z in range(8)] for yh in range(2) for core in range(2)]

    feat = features.transpose(1, 0, 2)
    ends = first(feat, short_filter, decay_rate)
    ends = lax.all_to_all(ends, "ctx", 0, 0, tiled=True)
    ctx = index // 16
    rate = lax.dynamic_slice(decay_rate, (ctx // 4 * 2, ctx % 4 * 128), (2, 128))
    ends, weight, halo, rate = tie((ends, weight, halo, rate))
    weights = lax.all_gather(weight, "ctx", axis_index_groups=along_z)
    incoming = lax.all_to_all(carry(ends, rate), "ctx", 0, 0, tiled=True).reshape(64, 128)

    query, drive, half = middle(feat, halo.transpose(1, 0, 2), short_filter, decay_rate)
    gain = residue * jnp.sqrt(-jnp.expm1(-2.0 * decay_rate))
    gated = back(query, drive, half, incoming, decay_rate, gain, skip[None])

    both = jnp.concatenate([gated, other_core(gated, others)], axis=0)
    beyond = move(both, axes, lambda yh, z, core, x, yl: (1 - yh, z, core, x, yl), mine)
    line = jnp.concatenate([both, beyond], axis=0)
    fwd = move(line, axes, along("x", 1), mine)
    bwd = move(line, axes, along("x", -1), mine)
    half_rows = line.shape[0] // 2
    hf = move(fwd[:half_rows], axes, along("x", 1), others)
    hb = move(bwd[half_rows:], axes, along("x", -1), others)

    own = x % 2 == core
    low = jnp.where(own, x // 2, (x + 3) % 4 // 2)
    high = jnp.where(own, 1 - x // 2, (x + 1) % 4 // 2)
    table = jnp.stack([own.astype(jnp.int32), yl, low, high]).astype(jnp.int32)
    keep, send = mix(table, line, fwd, bwd, hf, hb, weights)

    blocks = keep + other_core(send)
    parts = [move(blocks[d].astype(jnp.bfloat16), axes, along("yl", d)) for d in range(1, 4)]
    total = blocks[0] + sum(part.astype(jnp.float32) for part in parts)
    return move(
        total.astype(jnp.bfloat16), axes, lambda yh, z, core, x, yl: (yh ^ (yl // 2), z, core, yh * 2 + yl % 2, x)
    )


def shards(*arguments):
    return body(*arguments, AXES, first, carry, middle, back, mix)


def solution(mesh):
    in_specs = (
        P("ctx", None, "tp"),
        P(None, None, "tp"),
        P(None, "tp"),
        P(None, "tp"),
        P("tp"),
        P("tp", "ctx"),
    )
    return jax.shard_map(shards, mesh=mesh, in_specs=in_specs, out_specs=P("ctx", "tp"), check_vma=False)
```

```python
import functools

import jax
import jax.numpy as jnp
from jax import lax
from jax.experimental import pallas as pl
from jax.experimental.pallas import tpu as pltpu
from jax.sharding import PartitionSpec as P

AXES = ("ctx", "tp")
EVERY = [
    (yh, z, core, x, yl)
    for yh in range(2)
    for z in range(8)
    for core in range(2)
    for x in range(4)
    for yl in range(4)
]


def flat(yh, z, core, x, yl):
    return ((yh * 8 + z) * 2 + core) * 16 + x * 4 + yl


def move(value, axes, target, sends=lambda *place: True):
    pairs = [(flat(*p), flat(*target(*p))) for p in EVERY if sends(*p)]
    return lax.ppermute(value, axes, pairs)


def from_behind(value, axes, by):
    pairs = [(i, i + by * 16) for i in range(512) if i + by * 16 < 512]
    return lax.ppermute(value, axes, pairs)


VMEM = pl.BlockSpec(memory_space=pltpu.VMEM)
SMEM = pl.BlockSpec(memory_space=pltpu.SMEM)


def spread(ref, value):
    rows = value.shape[0]
    for half in range(2):
        for part in range(4):
            ref[pl.ds(half * 4 + part, rows, stride=8), :] = value[:, part * 128 : part * 128 + 128]


def first_kernel(feat_ref, taps_ref, rate_ref, out_ref, ext, drive_ref, lam):
    both = []
    sides = []
    for f in (1, 2):
        taps = [taps_ref[j, f : f + 1, :] for j in range(3)]
        ext[8:136, :] = feat_ref[f].astype(jnp.float32)
        ext[0:8, :] = jnp.zeros((8, 512), jnp.float32)
        total = taps[0] * ext[8:136, :] + taps[1] * ext[7:135, :] + taps[2] * ext[6:134, :]
        both.append(total)
        last = ext[135:136, :]
        sides.append((total[0:1], total[1:2], taps[1] * last + taps[2] * ext[134:135, :], taps[2] * last))
    drive = both[0] * both[1]
    side = jnp.concatenate([sides[0][0], sides[1][0], sides[0][1], sides[1][1], sides[0][2], sides[1][2], sides[0][3], sides[1][3]], axis=0)
    pack_positions(drive_ref, drive)
    spread(lam, jnp.exp(-rate_ref[...]))
    lams = [lam[m * 8 : m * 8 + 8, :] for m in range(16)]

    def step(t, states):
        now = drive_ref[pl.ds(pl.multiple_of(t * 8, 8), 8), :]
        return tuple(a * s + now for a, s in zip(lams, states))

    states = lax.fori_loop(0, 64, step, tuple(jnp.zeros((8, 128), jnp.float32) for _ in range(16)), unroll=4)
    spread(lam, jnp.exp(-64.0 * rate_ref[...]))
    for part in range(4):
        for pair in range(8):
            out_ref[pair * 4 + part, 8:16, :] = side[:, part * 128 : part * 128 + 128]
    for m in range(16):
        end = states[m] + pltpu.roll(lam[m * 8 : m * 8 + 8, :] * states[m], 4, 0)
        for part in range(4):
            out_ref[m // 2 * 4 + part, m % 2 : m % 2 + 1, :] = end[4 + part : 5 + part]


def carry_kernel(ends_ref, rate_ref, out_ref):
    rate = rate_ref[...]
    whole, late, later = jnp.exp(-128.0 * rate), jnp.exp(-127.0 * rate), jnp.exp(-126.0 * rate)
    state = jnp.zeros((2, 128), jnp.float32)
    for k in range(32):
        out_ref[k] = state
        end = ends_ref[k, 0:2, :]
        if k > 0:
            here, before = ends_ref[k, 8:12, :], ends_ref[k - 1, 12:16, :]
            full = here + before
            end = end + late * (full[0:1] * full[1:2] - here[0:1] * here[1:2])
            end = end + later * (full[2:3] * full[3:4] - here[2:3] * here[3:4])
        state = whole * state + end


def pack_positions(ref, drive):
    for half in range(2):
        for part in range(4):
            ref[pl.ds(half * 4 + part, 64, stride=8), :] = drive[
                half * 64 : half * 64 + 64, part * 128 : part * 128 + 128
            ]


def middle_kernel(feat_ref, halo_ref, taps_ref, rate_ref, query_ref, drive_ref, half_ref, ext, lam):
    filtered = []
    for f in range(3):
        ext[8:136, :] = feat_ref[f].astype(jnp.float32)
        ext[6:8, :] = halo_ref[f].astype(jnp.float32)
        total = taps_ref[0, f : f + 1, :] * ext[8:136, :]
        total = total + taps_ref[1, f : f + 1, :] * ext[7:135, :]
        filtered.append(total + taps_ref[2, f : f + 1, :] * ext[6:134, :])
    query_ref[...] = filtered[0]
    pack_positions(drive_ref, filtered[1] * filtered[2])
    spread(lam, jnp.exp(-rate_ref[...]))
    lams = [lam[m * 8 : m * 8 + 8, :] for m in range(16)]

    def step(t, states):
        now = drive_ref[pl.ds(pl.multiple_of(t * 8, 8), 8), :]
        return tuple(a * s + now for a, s in zip(lams, states))

    states = lax.fori_loop(0, 64, step, tuple(jnp.zeros((8, 128), jnp.float32) for _ in range(16)), unroll=4)
    for m in range(16):
        half_ref[m * 8 : m * 8 + 8, :] = states[m]


def back_kernel(query_ref, drive_ref, half_ref, in_ref, rate_ref, gain_ref, skip_ref, out_ref, lam, gain, skip, resp):
    spread(gain, gain_ref[...])
    spread(lam, jnp.exp(-64.0 * rate_ref[...]))
    states = []
    for m in range(16):
        rows = slice(m * 8, m * 8 + 8)
        came = in_ref[pl.ds(m // 2 * 8 + m % 2, 4, stride=2), :]
        later = lam[m * 8 : m * 8 + 4, :] * came + half_ref[m * 8 : m * 8 + 4, :]
        states.append(jnp.concatenate([came, later], axis=0))
    spread(lam, jnp.exp(-rate_ref[...]))
    spread(skip, skip_ref[...])
    lams = [lam[m * 8 : m * 8 + 8, :] for m in range(16)]
    gains = [gain[m * 8 : m * 8 + 8, :] for m in range(16)]
    direct = skip[...]

    def step(t, states):
        rows = pl.ds(pl.multiple_of(t * 8, 8), 8)
        now = drive_ref[rows, :]
        states = tuple(a * s + now for a, s in zip(lams, states))
        sums = [direct * now, None, None, None]
        for m in range(16):
            term = gains[m] * states[m]
            sums[m % 4] = term if sums[m % 4] is None else sums[m % 4] + term
        resp[rows, :] = (sums[0] + sums[1]) + (sums[2] + sums[3])
        return states

    lax.fori_loop(0, 64, step, tuple(states), unroll=2)
    for half in range(2):
        for part in range(4):
            rows, cols = slice(half * 64, half * 64 + 64), slice(part * 128, part * 128 + 128)
            out_ref[rows, cols] = (query_ref[rows, cols] * resp[pl.ds(half * 4 + part, 64, stride=8), :]).astype(jnp.bfloat16)


def mix_kernel(table_ref, *refs):
    line, fwd, bwd, hf, hb, weights = refs[:6]
    keep_ref, send_ref, g, w, g_sem, w_sem = refs[6:]
    own = table_ref[0] == 1
    low, high = table_ref[1], table_ref[2]

    def from_own():
        return [
            pltpu.make_async_copy(line, g.at[low], g_sem.at[0]),
            pltpu.make_async_copy(hf, g.at[high, pl.ds(0, 256)], g_sem.at[1]),
            pltpu.make_async_copy(hb, g.at[high, pl.ds(256, 256)], g_sem.at[2]),
        ]

    def from_others():
        return [
            pltpu.make_async_copy(fwd, g.at[low], g_sem.at[0]),
            pltpu.make_async_copy(bwd, g.at[high], g_sem.at[1]),
        ]

    @pl.when(own)
    def _():
        for copy in from_own():
            copy.start()

    @pl.when(jnp.logical_not(own))
    def _():
        for copy in from_others():
            copy.start()

    loads = [pltpu.make_async_copy(weights.at[i], w.at[i], w_sem.at[i]) for i in range(8)]
    for copy in loads:
        copy.start()

    @pl.when(own)
    def _():
        for copy in from_own():
            copy.wait()

    @pl.when(jnp.logical_not(own))
    def _():
        for copy in from_others():
            copy.wait()

    for i in range(4):
        loads[2 * i].wait()
        loads[2 * i + 1].wait()
        part = jnp.dot(g[0], w[2 * i], preferred_element_type=jnp.float32)
        part = part + jnp.dot(g[1], w[2 * i + 1], preferred_element_type=jnp.float32)
        cols = slice(i % 2 * 256, i % 2 * 256 + 256)
        for far in range(2):
            keep_ref[far * 2 + i // 2, :, cols] = part[far * 256 : far * 256 + 128]
            send_ref[far * 2 + i // 2, :, cols] = part[far * 256 + 128 : far * 256 + 256]


TINY = pl.CostEstimate(flops=1, bytes_accessed=1, transcendentals=0)
F32 = jnp.float32


def first(feat, taps, rate):
    return pl.pallas_call(
        first_kernel,
        out_shape=jax.ShapeDtypeStruct((32, 16, 128), F32),
        in_specs=[VMEM] * 3,
        out_specs=VMEM,
        scratch_shapes=[pltpu.VMEM((136, 512), F32), pltpu.VMEM((512, 128), F32), pltpu.VMEM((128, 128), F32)],
        cost_estimate=TINY,
        name="first",
    )(feat, taps, rate)


def carry(ends, rate):
    return pl.pallas_call(
        carry_kernel,
        out_shape=jax.ShapeDtypeStruct((32, 2, 128), F32),
        in_specs=[VMEM] * 2,
        out_specs=VMEM,
        cost_estimate=TINY,
        name="carry",
    )(ends, rate)


def middle(feat, halo, taps, rate):
    return pl.pallas_call(
        middle_kernel,
        out_shape=(
            jax.ShapeDtypeStruct((128, 512), F32),
            jax.ShapeDtypeStruct((512, 128), F32),
            jax.ShapeDtypeStruct((128, 128), F32),
        ),
        in_specs=[VMEM] * 4,
        out_specs=(VMEM,) * 3,
        scratch_shapes=[pltpu.VMEM((136, 512), F32), pltpu.VMEM((128, 128), F32)],
        cost_estimate=TINY,
        name="middle",
    )(feat, halo, taps, rate)


def back(query, drive, half, incoming, rate, gain, skip):
    return pl.pallas_call(
        back_kernel,
        out_shape=jax.ShapeDtypeStruct((128, 512), jnp.bfloat16),
        in_specs=[VMEM] * 7,
        out_specs=VMEM,
        scratch_shapes=[pltpu.VMEM((128, 128), F32)] * 2 + [pltpu.VMEM((8, 128), F32), pltpu.VMEM((512, 128), F32)],
        cost_estimate=TINY,
        name="back",
    )(query, drive, half, incoming, rate, gain, skip)


def mix(table, *operands):
    out = jax.ShapeDtypeStruct((4, 128, 512), jnp.float32)
    return pl.pallas_call(
        mix_kernel,
        out_shape=(out, out),
        in_specs=[SMEM] + [pl.BlockSpec(memory_space=pl.ANY)] * len(operands),
        out_specs=(VMEM, VMEM),
        scratch_shapes=[
            pltpu.VMEM((2, 512, 512), jnp.bfloat16),
            pltpu.VMEM((8, 512, 256), jnp.bfloat16),
            pltpu.SemaphoreType.DMA((3,)),
            pltpu.SemaphoreType.DMA((8,)),
        ],
        compiler_params=pltpu.CompilerParams(vmem_limit_bytes=60 * 1024 * 1024),
        cost_estimate=pl.CostEstimate(flops=1_100_000_000, bytes_accessed=7_000_000, transcendentals=0),
        name="mix",
    )(table, *operands)


def body(features, short_filter, decay_rate, residue, skip, out_weight, axes, first, carry, middle, back, mix):
    positions = features.shape[0]
    index = lax.axis_index(axes)
    x, core = index // 4 % 4, index // 16 % 2

    halo = from_behind(features[positions - 2 :], axes, 1)

    tie = lax.optimization_barrier
    def place(yh, z, core, x, yl):
        return yh, z // 4 * 4 + core * 2 + x // 2, x % 2, z % 4, yl

    def along(axis, by):
        def target(yh, z, core, x, yl):
            if axis == "z":
                return yh, (z + by) % 8, core, x, yl
            if axis == "x":
                return yh, z, core, (x + by) % 4, yl
            return yh, z, core, x, (yl + by) % 4

        return target

    def mine(yh, z, core, x, yl):
        return x % 2 == core

    def others(yh, z, core, x, yl):
        return x % 2 != core

    def other_core(value, sends=lambda *place: True):
        return move(value, axes, lambda yh, z, core, x, yl: (yh, z, 1 - core, x, yl), sends)

    weight = move(out_weight, axes, place)
    along_z = [[(yh * 8 + z) * 2 + core for z in range(8)] for yh in range(2) for core in range(2)]

    feat = features.transpose(1, 0, 2)
    ends = first(feat, short_filter, decay_rate)
    ends = lax.all_to_all(ends, "ctx", 0, 0, tiled=True)
    ctx = index // 16
    rate = lax.dynamic_slice(decay_rate, (ctx // 4 * 2, ctx % 4 * 128), (2, 128))
    query, drive, half = middle(feat, halo.transpose(1, 0, 2), short_filter, decay_rate)
    gain = residue * jnp.sqrt(-jnp.expm1(-2.0 * decay_rate))
    ends, rate, query, drive, half, gain = tie((ends, rate, query, drive, half, gain))
    carried, weight = tie((carry(ends, rate), weight))
    incoming = lax.all_to_all(carried, "ctx", 0, 0, tiled=True).reshape(64, 128)
    copies = jnp.broadcast_to(weight[None], (8,) + weight.shape)
    weights = lax.all_to_all(copies, "ctx", 0, 0, axis_index_groups=along_z, tiled=True)

    gated = back(query, drive, half, incoming, decay_rate, gain, skip[None])

    both = jnp.concatenate([gated, other_core(gated, others)], axis=0)
    beyond = move(both, axes, lambda yh, z, core, x, yl: (1 - yh, z, core, x, yl), mine)
    line = jnp.concatenate([both, beyond], axis=0)
    fwd = move(line, axes, along("x", 1), mine)
    bwd = move(line, axes, along("x", -1), mine)
    fwd, bwd, weights = tie((fwd, bwd, weights))
    half_rows = line.shape[0] // 2
    hf = move(fwd[:half_rows], axes, along("x", 1), others)
    hb = move(bwd[half_rows:], axes, along("x", -1), others)

    own = x % 2 == core
    low = jnp.where(own, x // 2, (x + 3) % 4 // 2)
    high = jnp.where(own, 1 - x // 2, (x + 1) % 4 // 2)
    table = jnp.stack([own.astype(jnp.int32), low, high]).astype(jnp.int32)
    keep, send = mix(table, line, fwd, bwd, hf, hb, weights)

    blocks = (keep + other_core(send)).astype(jnp.bfloat16)
    along_yl = [[x * 4 + yl for yl in range(4)] for x in range(4)]
    blocks = lax.all_to_all(blocks, "tp", 0, 0, axis_index_groups=along_yl, tiled=True)
    total = jnp.sum(blocks.astype(jnp.float32), axis=0)
    return move(
        total.astype(jnp.bfloat16), axes, lambda yh, z, core, x, yl: (yh ^ (yl // 2), z, core, yh * 2 + yl % 2, x)
    )


def shards(*arguments):
    return body(*arguments, AXES, first, carry, middle, back, mix)


def solution(mesh):
    in_specs = (
        P("ctx", None, "tp"),
        P(None, None, "tp"),
        P(None, "tp"),
        P(None, "tp"),
        P("tp"),
        P("tp", "ctx"),
    )
    return jax.shard_map(shards, mesh=mesh, in_specs=in_specs, out_specs=P("ctx", "tp"), check_vma=False)
```

```python
import functools

import jax
import jax.numpy as jnp
from jax import lax
from jax.experimental import pallas as pl
from jax.experimental.pallas import tpu as pltpu
from jax.sharding import PartitionSpec as P

AXES = ("ctx", "tp")
EVERY = [
    (yh, z, core, x, yl)
    for yh in range(2)
    for z in range(8)
    for core in range(2)
    for x in range(4)
    for yl in range(4)
]


def flat(yh, z, core, x, yl):
    return ((yh * 8 + z) * 2 + core) * 16 + x * 4 + yl


def move(value, axes, target, sends=lambda *place: True):
    pairs = [(flat(*p), flat(*target(*p))) for p in EVERY if sends(*p)]
    return lax.ppermute(value, axes, pairs)


def from_behind(value, axes, by):
    pairs = [(i, i + by * 16) for i in range(512) if i + by * 16 < 512]
    return lax.ppermute(value, axes, pairs)


VMEM = pl.BlockSpec(memory_space=pltpu.VMEM)
SMEM = pl.BlockSpec(memory_space=pltpu.SMEM)


def spread(ref, value):
    rows = value.shape[0]
    for half in range(2):
        for part in range(4):
            ref[pl.ds(half * 4 + part, rows, stride=8), :] = value[:, part * 128 : part * 128 + 128]


def first_kernel(feat_ref, taps_ref, rate_ref, out_ref, ext, drive_ref, lam):
    both = []
    sides = []
    for f in (1, 2):
        taps = [taps_ref[j, f : f + 1, :] for j in range(3)]
        ext[8:136, :] = feat_ref[f].astype(jnp.float32)
        ext[0:8, :] = jnp.zeros((8, 512), jnp.float32)
        total = taps[0] * ext[8:136, :] + taps[1] * ext[7:135, :] + taps[2] * ext[6:134, :]
        both.append(total)
        last = ext[135:136, :]
        sides.append((total[0:1], total[1:2], taps[1] * last + taps[2] * ext[134:135, :], taps[2] * last))
    drive = both[0] * both[1]
    side = jnp.concatenate([sides[0][0], sides[1][0], sides[0][1], sides[1][1], sides[0][2], sides[1][2], sides[0][3], sides[1][3]], axis=0)
    pack_positions(drive_ref, drive)
    spread(lam, jnp.exp(-rate_ref[...]))
    lams = [lam[m * 8 : m * 8 + 8, :] for m in range(16)]

    def step(t, states):
        now = drive_ref[pl.ds(pl.multiple_of(t * 8, 8), 8), :]
        return tuple(a * s + now for a, s in zip(lams, states))

    states = lax.fori_loop(0, 64, step, tuple(jnp.zeros((8, 128), jnp.float32) for _ in range(16)), unroll=4)
    spread(lam, jnp.exp(-64.0 * rate_ref[...]))
    for part in range(4):
        for pair in range(8):
            out_ref[pair * 4 + part, 8:16, :] = side[:, part * 128 : part * 128 + 128]
    for m in range(16):
        end = states[m] + pltpu.roll(lam[m * 8 : m * 8 + 8, :] * states[m], 4, 0)
        for part in range(4):
            out_ref[m // 2 * 4 + part, m % 2 : m % 2 + 1, :] = end[4 + part : 5 + part]


def carry_kernel(ends_ref, rate_ref, out_ref):
    rate = rate_ref[...]
    whole, late, later = jnp.exp(-128.0 * rate), jnp.exp(-127.0 * rate), jnp.exp(-126.0 * rate)
    state = jnp.zeros((2, 128), jnp.float32)
    for k in range(32):
        out_ref[k] = state
        end = ends_ref[k, 0:2, :]
        if k > 0:
            here, before = ends_ref[k, 8:12, :], ends_ref[k - 1, 12:16, :]
            full = here + before
            end = end + late * (full[0:1] * full[1:2] - here[0:1] * here[1:2])
            end = end + later * (full[2:3] * full[3:4] - here[2:3] * here[3:4])
        state = whole * state + end


def pack_positions(ref, drive):
    for half in range(2):
        for part in range(4):
            ref[pl.ds(half * 4 + part, 64, stride=8), :] = drive[
                half * 64 : half * 64 + 64, part * 128 : part * 128 + 128
            ]


def middle_kernel(feat_ref, halo_ref, taps_ref, rate_ref, query_ref, drive_ref, half_ref, ext, lam):
    filtered = []
    for f in range(3):
        ext[8:136, :] = feat_ref[f].astype(jnp.float32)
        ext[6:8, :] = halo_ref[f].astype(jnp.float32)
        total = taps_ref[0, f : f + 1, :] * ext[8:136, :]
        total = total + taps_ref[1, f : f + 1, :] * ext[7:135, :]
        filtered.append(total + taps_ref[2, f : f + 1, :] * ext[6:134, :])
    query_ref[...] = filtered[0]
    pack_positions(drive_ref, filtered[1] * filtered[2])
    spread(lam, jnp.exp(-rate_ref[...]))
    lams = [lam[m * 8 : m * 8 + 8, :] for m in range(16)]

    def step(t, states):
        now = drive_ref[pl.ds(pl.multiple_of(t * 8, 8), 8), :]
        return tuple(a * s + now for a, s in zip(lams, states))

    states = lax.fori_loop(0, 64, step, tuple(jnp.zeros((8, 128), jnp.float32) for _ in range(16)), unroll=4)
    for m in range(16):
        half_ref[m * 8 : m * 8 + 8, :] = states[m]


def back_kernel(query_ref, drive_ref, half_ref, in_ref, rate_ref, gain_ref, skip_ref, out_ref, lam, gain, skip, resp):
    spread(gain, gain_ref[...])
    spread(lam, jnp.exp(-64.0 * rate_ref[...]))
    states = []
    for m in range(16):
        rows = slice(m * 8, m * 8 + 8)
        came = in_ref[pl.ds(m // 2 * 8 + m % 2, 4, stride=2), :]
        later = lam[m * 8 : m * 8 + 4, :] * came + half_ref[m * 8 : m * 8 + 4, :]
        states.append(jnp.concatenate([came, later], axis=0))
    spread(lam, jnp.exp(-rate_ref[...]))
    spread(skip, skip_ref[...])
    lams = [lam[m * 8 : m * 8 + 8, :] for m in range(16)]
    gains = [gain[m * 8 : m * 8 + 8, :] for m in range(16)]
    direct = skip[...]

    def step(t, states):
        rows = pl.ds(pl.multiple_of(t * 8, 8), 8)
        now = drive_ref[rows, :]
        states = tuple(a * s + now for a, s in zip(lams, states))
        sums = [direct * now, None, None, None]
        for m in range(16):
            term = gains[m] * states[m]
            sums[m % 4] = term if sums[m % 4] is None else sums[m % 4] + term
        resp[rows, :] = (sums[0] + sums[1]) + (sums[2] + sums[3])
        return states

    lax.fori_loop(0, 64, step, tuple(states), unroll=2)
    for half in range(2):
        for part in range(4):
            rows, cols = slice(half * 64, half * 64 + 64), slice(part * 128, part * 128 + 128)
            out_ref[rows, cols] = (query_ref[rows, cols] * resp[pl.ds(half * 4 + part, 64, stride=8), :]).astype(jnp.bfloat16)


def mix_kernel(part, table_ref, line, fwd, bwd, hf, hb, weights, out_ref, g, w, g_sem, w_sem):
    own = table_ref[0] == 1
    yl = table_ref[1]

    def copies(pieces):
        made = []
        for far in range(2):
            for source, rows, block in pieces[far]:
                depth = pl.ds(pl.multiple_of(table_ref[block] * 512, 512), 512)
                target = g.at[pl.ds(far * 128, 128), depth]
                made.append(pltpu.make_async_copy(source.at[pl.ds(rows + part * 128, 128), :], target, g_sem.at[len(made)]))
        return made

    from_own = [[(line, 0, 2), (hf, 0, 3)], [(line, 256, 2), (hb, 0, 3)]]
    from_others = [[(fwd, 0, 2), (bwd, 0, 3)], [(fwd, 256, 2), (bwd, 256, 3)]]

    @pl.when(own)
    def _():
        for copy in copies(from_own):
            copy.start()

    @pl.when(jnp.logical_not(own))
    def _():
        for copy in copies(from_others):
            copy.start()

    loads = [pltpu.make_async_copy(weights.at[i], w.at[i], w_sem.at[i]) for i in range(4)]
    for copy in loads:
        copy.start()

    @pl.when(own)
    def _():
        for copy in copies(from_own):
            copy.wait()

    @pl.when(jnp.logical_not(own))
    def _():
        for copy in copies(from_others):
            copy.wait()

    for i in range(4):
        loads[i].wait()
        total = jnp.dot(g[...], w[i], preferred_element_type=jnp.float32)
        cols = slice(i % 2 * 256, i % 2 * 256 + 256)
        for far in range(2):
            d = lax.rem(far * 2 + i // 2 - yl + 4, 4)
            out_ref[d, :, cols] = total[far * 128 : far * 128 + 128]


TINY = pl.CostEstimate(flops=1, bytes_accessed=1, transcendentals=0)
F32 = jnp.float32


def first(feat, taps, rate):
    return pl.pallas_call(
        first_kernel,
        out_shape=jax.ShapeDtypeStruct((32, 16, 128), F32),
        in_specs=[VMEM] * 3,
        out_specs=VMEM,
        scratch_shapes=[pltpu.VMEM((136, 512), F32), pltpu.VMEM((512, 128), F32), pltpu.VMEM((128, 128), F32)],
        cost_estimate=TINY,
        name="first",
    )(feat, taps, rate)


def carry(ends, rate):
    return pl.pallas_call(
        carry_kernel,
        out_shape=jax.ShapeDtypeStruct((32, 2, 128), F32),
        in_specs=[VMEM] * 2,
        out_specs=VMEM,
        cost_estimate=TINY,
        name="carry",
    )(ends, rate)


def middle(feat, halo, taps, rate):
    return pl.pallas_call(
        middle_kernel,
        out_shape=(
            jax.ShapeDtypeStruct((128, 512), F32),
            jax.ShapeDtypeStruct((512, 128), F32),
            jax.ShapeDtypeStruct((128, 128), F32),
        ),
        in_specs=[VMEM] * 4,
        out_specs=(VMEM,) * 3,
        scratch_shapes=[pltpu.VMEM((136, 512), F32), pltpu.VMEM((128, 128), F32)],
        cost_estimate=TINY,
        name="middle",
    )(feat, halo, taps, rate)


def back(query, drive, half, incoming, rate, gain, skip):
    return pl.pallas_call(
        back_kernel,
        out_shape=jax.ShapeDtypeStruct((128, 512), jnp.bfloat16),
        in_specs=[VMEM] * 7,
        out_specs=VMEM,
        scratch_shapes=[pltpu.VMEM((128, 128), F32)] * 2 + [pltpu.VMEM((8, 128), F32), pltpu.VMEM((512, 128), F32)],
        cost_estimate=TINY,
        name="back",
    )(query, drive, half, incoming, rate, gain, skip)


def mix(part, table, *operands):
    return pl.pallas_call(
        functools.partial(mix_kernel, part),
        out_shape=jax.ShapeDtypeStruct((4, 128, 512), jnp.float32),
        in_specs=[SMEM] + [pl.BlockSpec(memory_space=pl.ANY)] * len(operands),
        out_specs=VMEM,
        scratch_shapes=[
            pltpu.VMEM((256, 1024), jnp.bfloat16),
            pltpu.VMEM((4, 1024, 256), jnp.bfloat16),
            pltpu.SemaphoreType.DMA((4,)),
            pltpu.SemaphoreType.DMA((4,)),
        ],
        compiler_params=pltpu.CompilerParams(vmem_limit_bytes=60 * 1024 * 1024),
        cost_estimate=pl.CostEstimate(flops=600_000_000, bytes_accessed=4_000_000, transcendentals=0),
        name=("keep", "send")[part],
    )(table, *operands)


def body(features, short_filter, decay_rate, residue, skip, out_weight, axes, first, carry, middle, back, mix):
    positions = features.shape[0]
    index = lax.axis_index(axes)
    yl, x, core = index % 4, index // 4 % 4, index // 16 % 2

    halo = from_behind(features[positions - 2 :], axes, 1)

    tie = lax.optimization_barrier
    def place(yh, z, core, x, yl):
        return yh, z // 4 * 4 + core * 2 + x // 2, x % 2, z % 4, yl

    def along(axis, by):
        def target(yh, z, core, x, yl):
            if axis == "z":
                return yh, (z + by) % 8, core, x, yl
            if axis == "x":
                return yh, z, core, (x + by) % 4, yl
            return yh, z, core, x, (yl + by) % 4

        return target

    def mine(yh, z, core, x, yl):
        return x % 2 == core

    def others(yh, z, core, x, yl):
        return x % 2 != core

    def other_core(value, sends=lambda *place: True):
        return move(value, axes, lambda yh, z, core, x, yl: (yh, z, 1 - core, x, yl), sends)

    weight = move(out_weight, axes, place)
    along_z = [[(yh * 8 + z) * 2 + core for z in range(8)] for yh in range(2) for core in range(2)]

    feat = features.transpose(1, 0, 2)
    ends = first(feat, short_filter, decay_rate)
    ends = lax.all_to_all(ends, "ctx", 0, 0, tiled=True)
    ctx = index // 16
    rate = lax.dynamic_slice(decay_rate, (ctx // 4 * 2, ctx % 4 * 128), (2, 128))
    ends, rate = tie((ends, rate))
    carried, weight, halo = tie((carry(ends, rate), weight, halo))
    weights = lax.all_gather(weight, "ctx", axis_index_groups=along_z)
    incoming = lax.all_to_all(carried, "ctx", 0, 0, tiled=True).reshape(64, 128)

    query, drive, half = middle(feat, halo.transpose(1, 0, 2), short_filter, decay_rate)
    gain = residue * jnp.sqrt(-jnp.expm1(-2.0 * decay_rate))
    gated = back(query, drive, half, incoming, decay_rate, gain, skip[None])

    both = jnp.concatenate([gated, other_core(gated, others)], axis=0)
    beyond = move(both, axes, lambda yh, z, core, x, yl: (1 - yh, z, core, x, yl), mine)
    line = jnp.concatenate([both, beyond], axis=0)
    fwd = move(line, axes, along("x", 1), mine)
    bwd = move(line, axes, along("x", -1), mine)
    half_rows = line.shape[0] // 2
    hf = move(fwd[:half_rows], axes, along("x", 1), others)
    hb = move(bwd[half_rows:], axes, along("x", -1), others)

    own = x % 2 == core
    low = jnp.where(own, x // 2, (x + 3) % 4 // 2)
    high = jnp.where(own, 1 - x // 2, (x + 1) % 4 // 2)
    table = jnp.stack([own.astype(jnp.int32), yl, low, high]).astype(jnp.int32)
    operands = (table, line, fwd, bwd, hf, hb, weights.reshape(4, 1024, 256))
    sent = other_core(mix(1, *operands))
    keep = mix(0, *operands)

    blocks = keep + sent
    parts = [move(blocks[d].astype(jnp.bfloat16), axes, along("yl", d)) for d in range(1, 4)]
    total = blocks[0] + sum(part.astype(jnp.float32) for part in parts)
    return move(
        total.astype(jnp.bfloat16), axes, lambda yh, z, core, x, yl: (yh ^ (yl // 2), z, core, yh * 2 + yl % 2, x)
    )


def shards(*arguments):
    return body(*arguments, AXES, first, carry, middle, back, mix)


def solution(mesh):
    in_specs = (
        P("ctx", None, "tp"),
        P(None, None, "tp"),
        P(None, "tp"),
        P(None, "tp"),
        P("tp"),
        P("tp", "ctx"),
    )
    return jax.shard_map(shards, mesh=mesh, in_specs=in_specs, out_specs=P("ctx", "tp"), check_vma=False)
```

```python
import functools

import jax
import jax.numpy as jnp
from jax import lax
from jax.experimental import pallas as pl
from jax.experimental.pallas import tpu as pltpu
from jax.sharding import PartitionSpec as P

AXES = ("ctx", "tp")
EVERY = [
    (yh, z, core, x, yl)
    for yh in range(2)
    for z in range(8)
    for core in range(2)
    for x in range(4)
    for yl in range(4)
]


def flat(yh, z, core, x, yl):
    return ((yh * 8 + z) * 2 + core) * 16 + x * 4 + yl


def move(value, axes, target, sends=lambda *place: True):
    pairs = [(flat(*p), flat(*target(*p))) for p in EVERY if sends(*p)]
    return lax.ppermute(value, axes, pairs)


def from_behind(value, axes, by):
    pairs = [(i, i + by * 16) for i in range(512) if i + by * 16 < 512]
    return lax.ppermute(value, axes, pairs)


VMEM = pl.BlockSpec(memory_space=pltpu.VMEM)
SMEM = pl.BlockSpec(memory_space=pltpu.SMEM)


def spread(ref, value):
    rows = value.shape[0]
    for half in range(2):
        for part in range(4):
            ref[pl.ds(half * 4 + part, rows, stride=8), :] = value[:, part * 128 : part * 128 + 128]


def first_kernel(feat_ref, taps_ref, rate_ref, out_ref, ext, drive_ref, lam):
    both = []
    sides = []
    for f in (1, 2):
        taps = [taps_ref[j, f : f + 1, :] for j in range(3)]
        ext[8:136, :] = feat_ref[f].astype(jnp.float32)
        ext[0:8, :] = jnp.zeros((8, 512), jnp.float32)
        total = taps[0] * ext[8:136, :] + taps[1] * ext[7:135, :] + taps[2] * ext[6:134, :]
        both.append(total)
        last = ext[135:136, :]
        sides.append((total[0:1], total[1:2], taps[1] * last + taps[2] * ext[134:135, :], taps[2] * last))
    drive = both[0] * both[1]
    side = jnp.concatenate([sides[0][0], sides[1][0], sides[0][1], sides[1][1], sides[0][2], sides[1][2], sides[0][3], sides[1][3]], axis=0)
    pack_positions(drive_ref, drive)
    spread(lam, jnp.exp(-rate_ref[...]))
    lams = [lam[m * 8 : m * 8 + 8, :] for m in range(16)]

    def step(t, states):
        now = drive_ref[pl.ds(pl.multiple_of(t * 8, 8), 8), :]
        return tuple(a * s + now for a, s in zip(lams, states))

    states = lax.fori_loop(0, 64, step, tuple(jnp.zeros((8, 128), jnp.float32) for _ in range(16)), unroll=4)
    spread(lam, jnp.exp(-64.0 * rate_ref[...]))
    for part in range(4):
        for pair in range(8):
            out_ref[pair * 4 + part, 8:16, :] = side[:, part * 128 : part * 128 + 128]
    for m in range(16):
        end = states[m] + pltpu.roll(lam[m * 8 : m * 8 + 8, :] * states[m], 4, 0)
        for part in range(4):
            out_ref[m // 2 * 4 + part, m % 2 : m % 2 + 1, :] = end[4 + part : 5 + part]


def carry_kernel(ends_ref, rate_ref, out_ref):
    rate = rate_ref[...]
    whole, late, later = jnp.exp(-128.0 * rate), jnp.exp(-127.0 * rate), jnp.exp(-126.0 * rate)
    state = jnp.zeros((2, 128), jnp.float32)
    for k in range(32):
        out_ref[k] = state
        end = ends_ref[k, 0:2, :]
        if k > 0:
            here, before = ends_ref[k, 8:12, :], ends_ref[k - 1, 12:16, :]
            full = here + before
            end = end + late * (full[0:1] * full[1:2] - here[0:1] * here[1:2])
            end = end + later * (full[2:3] * full[3:4] - here[2:3] * here[3:4])
        state = whole * state + end


def pack_positions(ref, drive):
    for half in range(2):
        for part in range(4):
            ref[pl.ds(half * 4 + part, 64, stride=8), :] = drive[
                half * 64 : half * 64 + 64, part * 128 : part * 128 + 128
            ]


def middle_kernel(feat_ref, halo_ref, taps_ref, rate_ref, query_ref, drive_ref, half_ref, ext, lam):
    filtered = []
    for f in range(3):
        ext[8:136, :] = feat_ref[f].astype(jnp.float32)
        ext[6:8, :] = halo_ref[f].astype(jnp.float32)
        total = taps_ref[0, f : f + 1, :] * ext[8:136, :]
        total = total + taps_ref[1, f : f + 1, :] * ext[7:135, :]
        filtered.append(total + taps_ref[2, f : f + 1, :] * ext[6:134, :])
    query_ref[...] = filtered[0]
    pack_positions(drive_ref, filtered[1] * filtered[2])
    spread(lam, jnp.exp(-rate_ref[...]))
    lams = [lam[m * 8 : m * 8 + 8, :] for m in range(16)]

    def step(t, states):
        now = drive_ref[pl.ds(pl.multiple_of(t * 8, 8), 8), :]
        return tuple(a * s + now for a, s in zip(lams, states))

    states = lax.fori_loop(0, 64, step, tuple(jnp.zeros((8, 128), jnp.float32) for _ in range(16)), unroll=4)
    for m in range(16):
        half_ref[m * 8 : m * 8 + 8, :] = states[m]


def back_kernel(query_ref, drive_ref, half_ref, in_ref, rate_ref, gain_ref, skip_ref, out_ref, lam, gain, skip, resp):
    spread(gain, gain_ref[...])
    spread(lam, jnp.exp(-64.0 * rate_ref[...]))
    states = []
    for m in range(16):
        rows = slice(m * 8, m * 8 + 8)
        came = in_ref[pl.ds(m // 2 * 8 + m % 2, 4, stride=2), :]
        later = lam[m * 8 : m * 8 + 4, :] * came + half_ref[m * 8 : m * 8 + 4, :]
        states.append(jnp.concatenate([came, later], axis=0))
    spread(lam, jnp.exp(-rate_ref[...]))
    spread(skip, skip_ref[...])
    lams = [lam[m * 8 : m * 8 + 8, :] for m in range(16)]
    gains = [gain[m * 8 : m * 8 + 8, :] for m in range(16)]
    direct = skip[...]

    def step(t, states):
        rows = pl.ds(pl.multiple_of(t * 8, 8), 8)
        now = drive_ref[rows, :]
        states = tuple(a * s + now for a, s in zip(lams, states))
        sums = [direct * now, None, None, None]
        for m in range(16):
            term = gains[m] * states[m]
            sums[m % 4] = term if sums[m % 4] is None else sums[m % 4] + term
        resp[rows, :] = (sums[0] + sums[1]) + (sums[2] + sums[3])
        return states

    lax.fori_loop(0, 64, step, tuple(states), unroll=2)
    for half in range(2):
        for part in range(4):
            rows, cols = slice(half * 64, half * 64 + 64), slice(part * 128, part * 128 + 128)
            out_ref[rows, cols] = (query_ref[rows, cols] * resp[pl.ds(half * 4 + part, 64, stride=8), :]).astype(jnp.bfloat16)


def mix_kernel(part, table_ref, line, fwd, bwd, hf, hb, weights, out_ref, g, g_sem):
    own = table_ref[0] == 1
    yl, x = table_ref[1], table_ref[4]

    def copies(pieces):
        made = []
        for far in range(2):
            for source, rows, block in pieces[far]:
                depth = pl.ds(pl.multiple_of(table_ref[block] * 512, 512), 512)
                target = g.at[pl.ds(far * 128, 128), depth]
                made.append(pltpu.make_async_copy(source.at[pl.ds(rows + part * 128, 128), :], target, g_sem.at[len(made)]))
        return made

    from_own = [[(line, 0, 2), (hf, 0, 3)], [(line, 256, 2), (hb, 0, 3)]]
    from_others = [[(fwd, 0, 2), (bwd, 0, 3)], [(fwd, 256, 2), (bwd, 256, 3)]]

    @pl.when(own)
    def _():
        for copy in copies(from_own):
            copy.start()

    @pl.when(jnp.logical_not(own))
    def _():
        for copy in copies(from_others):
            copy.start()

    @pl.when(own)
    def _():
        for copy in copies(from_own):
            copy.wait()

    @pl.when(jnp.logical_not(own))
    def _():
        for copy in copies(from_others):
            copy.wait()

    for i in range(4):
        total = jnp.dot(g[...], weights[i], preferred_element_type=jnp.float32)
        cols = slice(i % 2 * 256, i % 2 * 256 + 256)
        for far in range(2):
            d = lax.rem(lax.bitwise_xor(far * 2 + i // 2, x) - yl + 4, 4)
            out_ref[d, :, cols] = total[far * 128 : far * 128 + 128]


TINY = pl.CostEstimate(flops=1, bytes_accessed=1, transcendentals=0)
F32 = jnp.float32


def first(feat, taps, rate):
    return pl.pallas_call(
        first_kernel,
        out_shape=jax.ShapeDtypeStruct((32, 16, 128), F32),
        in_specs=[VMEM] * 3,
        out_specs=VMEM,
        scratch_shapes=[pltpu.VMEM((136, 512), F32), pltpu.VMEM((512, 128), F32), pltpu.VMEM((128, 128), F32)],
        cost_estimate=TINY,
        name="first",
    )(feat, taps, rate)


def carry(ends, rate):
    return pl.pallas_call(
        carry_kernel,
        out_shape=jax.ShapeDtypeStruct((32, 2, 128), F32),
        in_specs=[VMEM] * 2,
        out_specs=VMEM,
        cost_estimate=TINY,
        name="carry",
    )(ends, rate)


def middle(feat, halo, taps, rate):
    return pl.pallas_call(
        middle_kernel,
        out_shape=(
            jax.ShapeDtypeStruct((128, 512), F32),
            jax.ShapeDtypeStruct((512, 128), F32),
            jax.ShapeDtypeStruct((128, 128), F32),
        ),
        in_specs=[VMEM] * 4,
        out_specs=(VMEM,) * 3,
        scratch_shapes=[pltpu.VMEM((136, 512), F32), pltpu.VMEM((128, 128), F32)],
        cost_estimate=TINY,
        name="middle",
    )(feat, halo, taps, rate)


def back(query, drive, half, incoming, rate, gain, skip):
    return pl.pallas_call(
        back_kernel,
        out_shape=jax.ShapeDtypeStruct((128, 512), jnp.bfloat16),
        in_specs=[VMEM] * 7,
        out_specs=VMEM,
        scratch_shapes=[pltpu.VMEM((128, 128), F32)] * 2 + [pltpu.VMEM((8, 128), F32), pltpu.VMEM((512, 128), F32)],
        cost_estimate=TINY,
        name="back",
    )(query, drive, half, incoming, rate, gain, skip)


def mix(part, table, *operands):
    return pl.pallas_call(
        functools.partial(mix_kernel, part),
        out_shape=jax.ShapeDtypeStruct((4, 128, 512), jnp.float32),
        in_specs=[SMEM] + [pl.BlockSpec(memory_space=pl.ANY)] * 5 + [VMEM],
        out_specs=VMEM,
        scratch_shapes=[
            pltpu.VMEM((256, 1024), jnp.bfloat16),
            pltpu.SemaphoreType.DMA((4,)),
        ],
        compiler_params=pltpu.CompilerParams(vmem_limit_bytes=8 * 1024 * 1024),
        cost_estimate=pl.CostEstimate(flops=600_000_000, bytes_accessed=4_000_000, transcendentals=0),
        name=("keep", "send")[part],
    )(table, *operands)


def body(features, short_filter, decay_rate, residue, skip, out_weight, axes, first, carry, middle, back, mix):
    positions = features.shape[0]
    index = lax.axis_index(axes)
    yl, x, core = index % 4, index // 4 % 4, index // 16 % 2

    halo = from_behind(features[positions - 2 :], axes, 1)

    tie = lax.optimization_barrier
    def place(yh, z, core, x, yl):
        return yh, z // 4 * 4 + core * 2 + x // 2, x % 2, z % 4, yl

    def along(axis, by):
        def target(yh, z, core, x, yl):
            if axis == "z":
                return yh, (z + by) % 8, core, x, yl
            if axis == "x":
                return yh, z, core, (x + by) % 4, yl
            return yh, z, core, x, (yl + by) % 4

        return target

    def mine(yh, z, core, x, yl):
        return x % 2 == core

    def others(yh, z, core, x, yl):
        return x % 2 != core

    def other_core(value, sends=lambda *place: True):
        return move(value, axes, lambda yh, z, core, x, yl: (yh, z, 1 - core, x, yl), sends)

    weight = move(out_weight, axes, place)
    along_z = [[(yh * 8 + z) * 2 + core for z in range(8)] for yh in range(2) for core in range(2)]

    feat = features.transpose(1, 0, 2)
    ends = first(feat, short_filter, decay_rate)
    ends = lax.all_to_all(ends, "ctx", 0, 0, tiled=True)
    ctx = index // 16
    rate = lax.dynamic_slice(decay_rate, (ctx // 4 * 2, ctx % 4 * 128), (2, 128))
    ends, rate = tie((ends, rate))
    carried, weight, halo = tie((carry(ends, rate), weight, halo))
    weights = lax.all_gather(weight, "ctx", axis_index_groups=along_z)
    incoming = lax.all_to_all(carried, "ctx", 0, 0, tiled=True).reshape(64, 128)

    query, drive, half = middle(feat, halo.transpose(1, 0, 2), short_filter, decay_rate)
    gain = residue * jnp.sqrt(-jnp.expm1(-2.0 * decay_rate))
    gated = back(query, drive, half, incoming, decay_rate, gain, skip[None])

    both = jnp.concatenate([gated, other_core(gated, others)], axis=0)
    beyond = move(both, axes, lambda yh, z, core, x, yl: (1 - yh, z, core, x, yl), mine)
    line = jnp.concatenate([both, beyond], axis=0)
    fwd = move(line, axes, along("x", 1), mine)
    bwd = move(line, axes, along("x", -1), mine)
    half_rows = line.shape[0] // 2
    hf = move(fwd[:half_rows], axes, along("x", 1), others)
    hb = move(bwd[half_rows:], axes, along("x", -1), others)

    own = x % 2 == core
    low = jnp.where(own, x // 2, (x + 3) % 4 // 2)
    high = jnp.where(own, 1 - x // 2, (x + 1) % 4 // 2)
    table = jnp.stack([own.astype(jnp.int32), yl, low, high, x]).astype(jnp.int32)
    operands = (table, line, fwd, bwd, hf, hb, weights.reshape(4, 1024, 256))
    sent = other_core(mix(1, *operands))
    keep = mix(0, *operands)

    blocks = keep + sent
    parts = [move(blocks[d].astype(jnp.bfloat16), axes, along("yl", d)) for d in range(1, 4)]
    total = blocks[0] + sum(part.astype(jnp.float32) for part in parts)

    def home(yh, z, core, x, yl):
        block = yl ^ x
        return yh ^ (block // 2), z, core, yh * 2 + block % 2, x

    return move(total.astype(jnp.bfloat16), axes, home)


def shards(*arguments):
    return body(*arguments, AXES, first, carry, middle, back, mix)


def solution(mesh):
    in_specs = (
        P("ctx", None, "tp"),
        P(None, None, "tp"),
        P(None, "tp"),
        P(None, "tp"),
        P("tp"),
        P("tp", "ctx"),
    )
    return jax.shard_map(shards, mesh=mesh, in_specs=in_specs, out_specs=P("ctx", "tp"), check_vma=False)
```

```python
import functools

import jax
import jax.numpy as jnp
from jax import lax
from jax.experimental import pallas as pl
from jax.experimental.pallas import tpu as pltpu
from jax.sharding import PartitionSpec as P

AXES = ("ctx", "tp")
EVERY = [
    (yh, z, core, x, yl)
    for yh in range(2)
    for z in range(8)
    for core in range(2)
    for x in range(4)
    for yl in range(4)
]


def flat(yh, z, core, x, yl):
    return ((yh * 8 + z) * 2 + core) * 16 + x * 4 + yl


def move(value, axes, target, sends=lambda *place: True):
    pairs = [(flat(*p), flat(*target(*p))) for p in EVERY if sends(*p)]
    return lax.ppermute(value, axes, pairs)


VMEM = pl.BlockSpec(memory_space=pltpu.VMEM)
SMEM = pl.BlockSpec(memory_space=pltpu.SMEM)


def spread(ref, value):
    rows = value.shape[0]
    for half in range(2):
        for part in range(4):
            ref[pl.ds(half * 4 + part, rows, stride=8), :] = value[:, part * 128 : part * 128 + 128]


def first_kernel(feat_ref, taps_ref, rate_ref, out_ref, query_ref, drive_ref, half_ref, own_ref, ext, lam):
    totals = []
    sides = []
    for f in range(3):
        taps = [taps_ref[j, f : f + 1, :] for j in range(3)]
        ext[8:136, :] = feat_ref[f].astype(jnp.float32)
        ext[0:8, :] = jnp.zeros((8, 512), jnp.float32)
        total = taps[0] * ext[8:136, :] + taps[1] * ext[7:135, :] + taps[2] * ext[6:134, :]
        totals.append(total)
        last = ext[135:136, :]
        sides.append((total[0:1], total[1:2], taps[1] * last + taps[2] * ext[134:135, :], taps[2] * last))
    query_ref[...] = totals[0]
    own = [sides[1][0], sides[2][0], sides[1][1], sides[2][1]]
    side = jnp.concatenate(own + [sides[1][2], sides[2][2], sides[1][3], sides[2][3]], axis=0)
    for r in range(4):
        for part in range(4):
            own_ref[r * 4 + part : r * 4 + part + 1, :] = own[r][:, part * 128 : part * 128 + 128]
    pack_positions(drive_ref, totals[1] * totals[2])
    spread(lam, jnp.exp(-rate_ref[...]))
    lams = [lam[m * 8 : m * 8 + 8, :] for m in range(16)]

    def step(t, states):
        now = drive_ref[pl.ds(pl.multiple_of(t * 8, 8), 8), :]
        return tuple(a * s + now for a, s in zip(lams, states))

    states = lax.fori_loop(0, 64, step, tuple(jnp.zeros((8, 128), jnp.float32) for _ in range(16)), unroll=4)
    spread(lam, jnp.exp(-64.0 * rate_ref[...]))
    for part in range(4):
        cols = slice(part * 128, part * 128 + 128)
        for pair in range(8):
            out_ref[pair * 4 + part, 8:16, :] = side[:, cols]
            out_ref[pair * 4 + part, 2:3, :] = sides[0][2][:, cols]
            out_ref[pair * 4 + part, 3:4, :] = sides[0][3][:, cols]
    for m in range(16):
        half_ref[m * 8 : m * 8 + 8, :] = states[m]
        end = states[m] + pltpu.roll(lam[m * 8 : m * 8 + 8, :] * states[m], 4, 0)
        for part in range(4):
            out_ref[m // 2 * 4 + part, m % 2 : m % 2 + 1, :] = end[4 + part : 5 + part]


def carry_kernel(ends_ref, rate_ref, out_ref):
    rate = rate_ref[...]
    whole, late, later = jnp.exp(-128.0 * rate), jnp.exp(-127.0 * rate), jnp.exp(-126.0 * rate)
    state = jnp.zeros((2, 128), jnp.float32)
    for k in range(32):
        out_ref[k, 0:2, :] = state
        end = ends_ref[k, 0:2, :]
        if k == 0:
            out_ref[k, 2:8, :] = jnp.zeros((6, 128), jnp.float32)
        else:
            here, before = ends_ref[k, 8:12, :], ends_ref[k - 1, 12:16, :]
            out_ref[k, 2:6, :] = before
            out_ref[k, 6:8, :] = ends_ref[k - 1, 2:4, :]
            full = here + before
            end = end + late * (full[0:1] * full[1:2] - here[0:1] * here[1:2])
            end = end + later * (full[2:3] * full[3:4] - here[2:3] * here[3:4])
        state = whole * state + end


def pack_positions(ref, drive):
    for half in range(2):
        for part in range(4):
            ref[pl.ds(half * 4 + part, 64, stride=8), :] = drive[
                half * 64 : half * 64 + 64, part * 128 : part * 128 + 128
            ]


def back_kernel(
    query_ref, drive_ref, half_ref, own_ref, in_ref, rate_ref, gain_ref, skip_ref, out_ref, lam, late, later, gain, skip, resp
):
    spread(gain, gain_ref[...])
    spread(lam, jnp.exp(-64.0 * rate_ref[...]))
    spread(late, jnp.exp(-63.0 * rate_ref[...]))
    spread(later, jnp.exp(-62.0 * rate_ref[...]))
    own = [own_ref[r * 4 : r * 4 + 4, :] for r in range(4)]
    full = [own[r] + in_ref[pl.ds(2 + r, 4, stride=8), :] for r in range(4)]
    more = [full[0] * full[1] - own[0] * own[1], full[2] * full[3] - own[2] * own[3]]
    states = []
    for m in range(16):
        rows = slice(m * 8, m * 8 + 4)
        came = in_ref[pl.ds(m // 2 * 32 + m % 2, 4, stride=8), :]
        half = half_ref[rows, :] + late[rows, :] * more[0] + later[rows, :] * more[1]
        states.append(jnp.concatenate([came, lam[rows, :] * came + half], axis=0))
    spread(lam, jnp.exp(-rate_ref[...]))
    spread(skip, skip_ref[...])
    lams = [lam[m * 8 : m * 8 + 8, :] for m in range(16)]
    gains = [gain[m * 8 : m * 8 + 8, :] for m in range(16)]
    direct = skip[...]

    def advance(now, states):
        states = tuple(a * s + now for a, s in zip(lams, states))
        sums = [direct * now, None, None, None]
        for m in range(16):
            term = gains[m] * states[m]
            sums[m % 4] = term if sums[m % 4] is None else sums[m % 4] + term
        return (sums[0] + sums[1]) + (sums[2] + sums[3]), states

    states = tuple(states)
    for t in range(2):
        now = drive_ref[t * 8 : t * 8 + 8, :]
        now = now + jnp.concatenate([more[t], jnp.zeros((4, 128), jnp.float32)], axis=0)
        resp[t * 8 : t * 8 + 8, :], states = advance(now, states)

    def step(t, states):
        rows = pl.ds(pl.multiple_of(t * 8, 8), 8)
        resp[rows, :], states = advance(drive_ref[rows, :], states)
        return states

    lax.fori_loop(2, 64, step, states, unroll=2)
    row = lax.broadcasted_iota(jnp.int32, (64, 128), 0)
    for half in range(2):
        for part in range(4):
            rows, cols = slice(half * 64, half * 64 + 64), slice(part * 128, part * 128 + 128)
            query = query_ref[rows, cols]
            if half == 0:
                query = query + jnp.where(row == 0, in_ref[part * 8 + 6 : part * 8 + 7, :], 0.0)
                query = query + jnp.where(row == 1, in_ref[part * 8 + 7 : part * 8 + 8, :], 0.0)
            out_ref[rows, cols] = (query * resp[pl.ds(half * 4 + part, 64, stride=8), :]).astype(jnp.bfloat16)


def mix_kernel(part, table_ref, line, fwd, bwd, hf, hb, weights, out_ref, g, g_sem):
    own = table_ref[0] == 1
    yl, x = table_ref[1], table_ref[4]

    def copies(pieces):
        made = []
        for far in range(2):
            for source, rows, block in pieces[far]:
                depth = pl.ds(pl.multiple_of(table_ref[block] * 512, 512), 512)
                target = g.at[pl.ds(far * 128, 128), depth]
                made.append(pltpu.make_async_copy(source.at[pl.ds(rows + part * 128, 128), :], target, g_sem.at[len(made)]))
        return made

    from_own = [[(line, 0, 2), (hf, 0, 3)], [(line, 256, 2), (hb, 0, 3)]]
    from_others = [[(fwd, 0, 2), (bwd, 0, 3)], [(fwd, 256, 2), (bwd, 256, 3)]]

    @pl.when(own)
    def _():
        for copy in copies(from_own):
            copy.start()

    @pl.when(jnp.logical_not(own))
    def _():
        for copy in copies(from_others):
            copy.start()

    @pl.when(own)
    def _():
        for copy in copies(from_own):
            copy.wait()

    @pl.when(jnp.logical_not(own))
    def _():
        for copy in copies(from_others):
            copy.wait()

    for i in range(4):
        total = jnp.dot(g[...], weights[i], preferred_element_type=jnp.float32)
        cols = slice(i % 2 * 256, i % 2 * 256 + 256)
        for far in range(2):
            d = lax.rem(lax.bitwise_xor(far * 2 + i // 2, x) - yl + 4, 4)
            out_ref[d, :, cols] = total[far * 128 : far * 128 + 128]


TINY = pl.CostEstimate(flops=1, bytes_accessed=1, transcendentals=0)
F32 = jnp.float32


def first(feat, taps, rate):
    return pl.pallas_call(
        first_kernel,
        out_shape=(
            jax.ShapeDtypeStruct((32, 16, 128), F32),
            jax.ShapeDtypeStruct((128, 512), F32),
            jax.ShapeDtypeStruct((512, 128), F32),
            jax.ShapeDtypeStruct((128, 128), F32),
            jax.ShapeDtypeStruct((16, 128), F32),
        ),
        in_specs=[VMEM] * 3,
        out_specs=(VMEM,) * 5,
        scratch_shapes=[pltpu.VMEM((136, 512), F32), pltpu.VMEM((128, 128), F32)],
        cost_estimate=TINY,
        name="first",
    )(feat, taps, rate)


def carry(ends, rate):
    return pl.pallas_call(
        carry_kernel,
        out_shape=jax.ShapeDtypeStruct((32, 8, 128), F32),
        in_specs=[VMEM] * 2,
        out_specs=VMEM,
        cost_estimate=TINY,
        name="carry",
    )(ends, rate)


def back(query, drive, half, own, incoming, rate, gain, skip):
    return pl.pallas_call(
        back_kernel,
        out_shape=jax.ShapeDtypeStruct((128, 512), jnp.bfloat16),
        in_specs=[VMEM] * 8,
        out_specs=VMEM,
        scratch_shapes=[pltpu.VMEM((128, 128), F32)] * 4 + [pltpu.VMEM((8, 128), F32), pltpu.VMEM((512, 128), F32)],
        cost_estimate=TINY,
        name="back",
    )(query, drive, half, own, incoming, rate, gain, skip)


def mix(part, table, *operands):
    return pl.pallas_call(
        functools.partial(mix_kernel, part),
        out_shape=jax.ShapeDtypeStruct((4, 128, 512), jnp.float32),
        in_specs=[SMEM] + [pl.BlockSpec(memory_space=pl.ANY)] * 5 + [VMEM],
        out_specs=VMEM,
        scratch_shapes=[
            pltpu.VMEM((256, 1024), jnp.bfloat16),
            pltpu.SemaphoreType.DMA((4,)),
        ],
        compiler_params=pltpu.CompilerParams(vmem_limit_bytes=8 * 1024 * 1024),
        cost_estimate=pl.CostEstimate(flops=600_000_000, bytes_accessed=4_000_000, transcendentals=0),
        name=("keep", "send")[part],
    )(table, *operands)


def body(features, short_filter, decay_rate, residue, skip, out_weight, axes, first, carry, back, mix):
    index = lax.axis_index(axes)
    yl, x, core = index % 4, index // 4 % 4, index // 16 % 2

    tie = lax.optimization_barrier
    def place(yh, z, core, x, yl):
        return yh, z // 4 * 4 + core * 2 + x // 2, x % 2, z % 4, yl

    def along(axis, by):
        def target(yh, z, core, x, yl):
            if axis == "z":
                return yh, (z + by) % 8, core, x, yl
            if axis == "x":
                return yh, z, core, (x + by) % 4, yl
            return yh, z, core, x, (yl + by) % 4

        return target

    def mine(yh, z, core, x, yl):
        return x % 2 == core

    def others(yh, z, core, x, yl):
        return x % 2 != core

    def other_core(value, sends=lambda *place: True):
        return move(value, axes, lambda yh, z, core, x, yl: (yh, z, 1 - core, x, yl), sends)

    weight = move(out_weight, axes, place)
    along_z = [[(yh * 8 + z) * 2 + core for z in range(8)] for yh in range(2) for core in range(2)]

    feat = features.transpose(1, 0, 2)
    ends, query, drive, half, own = first(feat, short_filter, decay_rate)
    ends = lax.all_to_all(ends, "ctx", 0, 0, tiled=True)
    ctx = index // 16
    rate = lax.dynamic_slice(decay_rate, (ctx // 4 * 2, ctx % 4 * 128), (2, 128))
    gain = residue * jnp.sqrt(-jnp.expm1(-2.0 * decay_rate))
    ends, rate, gain = tie((ends, rate, gain))
    carried, weight = tie((carry(ends, rate), weight))
    weights = lax.all_gather(weight, "ctx", axis_index_groups=along_z)
    incoming = lax.all_to_all(carried, "ctx", 0, 0, tiled=True).reshape(256, 128)

    gated = back(query, drive, half, own, incoming, decay_rate, gain, skip[None])

    both = jnp.concatenate([gated, other_core(gated, others)], axis=0)
    beyond = move(both, axes, lambda yh, z, core, x, yl: (1 - yh, z, core, x, yl), mine)
    line = jnp.concatenate([both, beyond], axis=0)
    fwd = move(line, axes, along("x", 1), mine)
    bwd = move(line, axes, along("x", -1), mine)
    half_rows = line.shape[0] // 2
    hf = move(fwd[:half_rows], axes, along("x", 1), others)
    hb = move(bwd[half_rows:], axes, along("x", -1), others)

    matched = x % 2 == core
    low = jnp.where(matched, x // 2, (x + 3) % 4 // 2)
    high = jnp.where(matched, 1 - x // 2, (x + 1) % 4 // 2)
    table = jnp.stack([matched.astype(jnp.int32), yl, low, high, x]).astype(jnp.int32)
    operands = (table, line, fwd, bwd, hf, hb, weights.reshape(4, 1024, 256))
    sent = other_core(mix(1, *operands))
    keep = mix(0, *operands)

    blocks = keep + sent
    parts = [move(blocks[d].astype(jnp.bfloat16), axes, along("yl", d)) for d in range(1, 4)]
    total = blocks[0] + sum(part.astype(jnp.float32) for part in parts)

    def home(yh, z, core, x, yl):
        block = yl ^ x
        return yh ^ (block // 2), z, core, yh * 2 + block % 2, x

    return move(total.astype(jnp.bfloat16), axes, home)


def shards(*arguments):
    return body(*arguments, AXES, first, carry, back, mix)


def solution(mesh):
    in_specs = (
        P("ctx", None, "tp"),
        P(None, None, "tp"),
        P(None, "tp"),
        P(None, "tp"),
        P("tp"),
        P("tp", "ctx"),
    )
    return jax.shard_map(shards, mesh=mesh, in_specs=in_specs, out_specs=P("ctx", "tp"), check_vma=False)
```

```python
import functools

import jax
import jax.numpy as jnp
from jax import lax
from jax.experimental import pallas as pl
from jax.experimental.pallas import tpu as pltpu
from jax.sharding import PartitionSpec as P

AXES = ("ctx", "tp")
EVERY = [
    (yh, z, core, x, yl)
    for yh in range(2)
    for z in range(8)
    for core in range(2)
    for x in range(4)
    for yl in range(4)
]


def flat(yh, z, core, x, yl):
    return ((yh * 8 + z) * 2 + core) * 16 + x * 4 + yl


def move(value, axes, target, sends=lambda *place: True):
    pairs = [(flat(*p), flat(*target(*p))) for p in EVERY if sends(*p)]
    return lax.ppermute(value, axes, pairs)


VMEM = pl.BlockSpec(memory_space=pltpu.VMEM)
SMEM = pl.BlockSpec(memory_space=pltpu.SMEM)


def spread(ref, value):
    rows = value.shape[0]
    for half in range(2):
        for part in range(4):
            ref[pl.ds(half * 4 + part, rows, stride=8), :] = value[:, part * 128 : part * 128 + 128]


def first_kernel(feat_ref, taps_ref, rate_ref, out_ref, query_ref, drive_ref, half_ref, own_ref, ext, lam):
    totals = []
    sides = []
    for f in range(3):
        taps = [taps_ref[j, f : f + 1, :] for j in range(3)]
        ext[8:136, :] = feat_ref[f].astype(jnp.float32)
        ext[0:8, :] = jnp.zeros((8, 512), jnp.float32)
        total = taps[0] * ext[8:136, :] + taps[1] * ext[7:135, :] + taps[2] * ext[6:134, :]
        totals.append(total)
        last = ext[135:136, :]
        sides.append((total[0:1], total[1:2], taps[1] * last + taps[2] * ext[134:135, :], taps[2] * last))
    query_ref[...] = totals[0]
    own = [sides[1][0], sides[2][0], sides[1][1], sides[2][1]]
    side = jnp.concatenate(own + [sides[1][2], sides[2][2], sides[1][3], sides[2][3]], axis=0)
    for r in range(4):
        for part in range(4):
            own_ref[r * 4 + part : r * 4 + part + 1, :] = own[r][:, part * 128 : part * 128 + 128]
    pack_positions(drive_ref, totals[1] * totals[2])
    spread(lam, jnp.exp(-rate_ref[...]))
    lams = [lam[m * 8 : m * 8 + 8, :] for m in range(16)]

    def step(t, states):
        now = drive_ref[pl.ds(pl.multiple_of(t * 8, 8), 8), :]
        return tuple(a * s + now for a, s in zip(lams, states))

    states = lax.fori_loop(0, 64, step, tuple(jnp.zeros((8, 128), jnp.float32) for _ in range(16)), unroll=4)
    spread(lam, jnp.exp(-64.0 * rate_ref[...]))
    for part in range(4):
        cols = slice(part * 128, part * 128 + 128)
        for pair in range(8):
            out_ref[pair * 4 + part, 8:16, :] = side[:, cols]
            out_ref[pair * 4 + part, 2:3, :] = sides[0][2][:, cols]
            out_ref[pair * 4 + part, 3:4, :] = sides[0][3][:, cols]
    for m in range(16):
        half_ref[m * 8 : m * 8 + 8, :] = states[m]
        end = states[m] + pltpu.roll(lam[m * 8 : m * 8 + 8, :] * states[m], 4, 0)
        for part in range(4):
            out_ref[m // 2 * 4 + part, m % 2 : m % 2 + 1, :] = end[4 + part : 5 + part]


def carry_kernel(ends_ref, rate_ref, out_ref):
    rate = rate_ref[...]
    whole, late, later = jnp.exp(-128.0 * rate), jnp.exp(-127.0 * rate), jnp.exp(-126.0 * rate)
    state = jnp.zeros((2, 128), jnp.float32)
    for k in range(32):
        out_ref[k, 0:2, :] = state
        end = ends_ref[k, 0:2, :]
        if k == 0:
            out_ref[k, 2:8, :] = jnp.zeros((6, 128), jnp.float32)
        else:
            here, before = ends_ref[k, 8:12, :], ends_ref[k - 1, 12:16, :]
            out_ref[k, 2:6, :] = before
            out_ref[k, 6:8, :] = ends_ref[k - 1, 2:4, :]
            full = here + before
            end = end + late * (full[0:1] * full[1:2] - here[0:1] * here[1:2])
            end = end + later * (full[2:3] * full[3:4] - here[2:3] * here[3:4])
        state = whole * state + end


def pack_positions(ref, drive):
    for half in range(2):
        for part in range(4):
            ref[pl.ds(half * 4 + part, 64, stride=8), :] = drive[
                half * 64 : half * 64 + 64, part * 128 : part * 128 + 128
            ]


def back_kernel(
    query_ref, drive_ref, half_ref, own_ref, in_ref, rate_ref, gain_ref, skip_ref, out_ref, lam, late, later, gain, skip, resp
):
    spread(gain, gain_ref[...])
    spread(lam, jnp.exp(-64.0 * rate_ref[...]))
    spread(late, jnp.exp(-63.0 * rate_ref[...]))
    spread(later, jnp.exp(-62.0 * rate_ref[...]))
    own = [own_ref[r * 4 : r * 4 + 4, :] for r in range(4)]
    full = [own[r] + in_ref[pl.ds(2 + r, 4, stride=8), :] for r in range(4)]
    more = [full[0] * full[1] - own[0] * own[1], full[2] * full[3] - own[2] * own[3]]
    states = []
    for m in range(16):
        rows = slice(m * 8, m * 8 + 4)
        came = in_ref[pl.ds(m // 2 * 32 + m % 2, 4, stride=8), :]
        half = half_ref[rows, :] + late[rows, :] * more[0] + later[rows, :] * more[1]
        states.append(jnp.concatenate([came, lam[rows, :] * came + half], axis=0))
    spread(lam, jnp.exp(-rate_ref[...]))
    spread(skip, skip_ref[...])
    lams = [lam[m * 8 : m * 8 + 8, :] for m in range(16)]
    gains = [gain[m * 8 : m * 8 + 8, :] for m in range(16)]
    direct = skip[...]

    def advance(now, states):
        states = tuple(a * s + now for a, s in zip(lams, states))
        sums = [direct * now, None, None, None]
        for m in range(16):
            term = gains[m] * states[m]
            sums[m % 4] = term if sums[m % 4] is None else sums[m % 4] + term
        return (sums[0] + sums[1]) + (sums[2] + sums[3]), states

    states = tuple(states)
    for t in range(2):
        now = drive_ref[t * 8 : t * 8 + 8, :]
        now = now + jnp.concatenate([more[t], jnp.zeros((4, 128), jnp.float32)], axis=0)
        resp[t * 8 : t * 8 + 8, :], states = advance(now, states)

    def step(t, states):
        rows = pl.ds(pl.multiple_of(t * 8, 8), 8)
        resp[rows, :], states = advance(drive_ref[rows, :], states)
        return states

    lax.fori_loop(2, 64, step, states, unroll=2)
    row = lax.broadcasted_iota(jnp.int32, (64, 128), 0)
    for half in range(2):
        for part in range(4):
            rows, cols = slice(half * 64, half * 64 + 64), slice(part * 128, part * 128 + 128)
            query = query_ref[rows, cols]
            if half == 0:
                query = query + jnp.where(row == 0, in_ref[part * 8 + 6 : part * 8 + 7, :], 0.0)
                query = query + jnp.where(row == 1, in_ref[part * 8 + 7 : part * 8 + 8, :], 0.0)
            out_ref[rows, cols] = (query * resp[pl.ds(half * 4 + part, 64, stride=8), :]).astype(jnp.bfloat16)


def mix_kernel(part, table_ref, line, fwd, bwd, hf, hb, weights, out_ref, g, g_sem):
    own = table_ref[0] == 1
    yl, x = table_ref[1], table_ref[4]

    def copies(pieces):
        made = []
        for far in range(2):
            for source, rows, block in pieces[far]:
                depth = pl.ds(pl.multiple_of(table_ref[block] * 512, 512), 512)
                target = g.at[pl.ds(far * 128, 128), depth]
                made.append(pltpu.make_async_copy(source.at[pl.ds(rows + part * 128, 128), :], target, g_sem.at[len(made)]))
        return made

    from_own = [[(line, 0, 2), (hf, 0, 3)], [(line, 256, 2), (hb, 0, 3)]]
    from_others = [[(fwd, 0, 2), (bwd, 0, 3)], [(fwd, 256, 2), (bwd, 256, 3)]]

    @pl.when(own)
    def _():
        for copy in copies(from_own):
            copy.start()

    @pl.when(jnp.logical_not(own))
    def _():
        for copy in copies(from_others):
            copy.start()

    @pl.when(own)
    def _():
        for copy in copies(from_own):
            copy.wait()

    @pl.when(jnp.logical_not(own))
    def _():
        for copy in copies(from_others):
            copy.wait()

    for i in range(4):
        total = jnp.dot(g[...], weights[i], preferred_element_type=jnp.float32)
        cols = slice(i % 2 * 256, i % 2 * 256 + 256)
        for far in range(2):
            d = lax.rem(lax.bitwise_xor(far * 2 + i // 2, x) - yl + 4, 4)
            out_ref[d, :, cols] = total[far * 128 : far * 128 + 128]


TINY = pl.CostEstimate(flops=1, bytes_accessed=1, transcendentals=0)
F32 = jnp.float32


def first(feat, taps, rate):
    return pl.pallas_call(
        first_kernel,
        out_shape=(
            jax.ShapeDtypeStruct((32, 16, 128), F32),
            jax.ShapeDtypeStruct((128, 512), F32),
            jax.ShapeDtypeStruct((512, 128), F32),
            jax.ShapeDtypeStruct((128, 128), F32),
            jax.ShapeDtypeStruct((16, 128), F32),
        ),
        in_specs=[VMEM] * 3,
        out_specs=(VMEM,) * 5,
        scratch_shapes=[pltpu.VMEM((136, 512), F32), pltpu.VMEM((128, 128), F32)],
        cost_estimate=TINY,
        name="first",
    )(feat, taps, rate)


def carry(ends, rate):
    return pl.pallas_call(
        carry_kernel,
        out_shape=jax.ShapeDtypeStruct((32, 8, 128), F32),
        in_specs=[VMEM] * 2,
        out_specs=VMEM,
        cost_estimate=TINY,
        name="carry",
    )(ends, rate)


def back(query, drive, half, own, incoming, rate, gain, skip):
    return pl.pallas_call(
        back_kernel,
        out_shape=jax.ShapeDtypeStruct((128, 512), jnp.bfloat16),
        in_specs=[VMEM] * 8,
        out_specs=VMEM,
        scratch_shapes=[pltpu.VMEM((128, 128), F32)] * 4 + [pltpu.VMEM((8, 128), F32), pltpu.VMEM((512, 128), F32)],
        cost_estimate=TINY,
        name="back",
    )(query, drive, half, own, incoming, rate, gain, skip)


def mix(part, table, *operands):
    return pl.pallas_call(
        functools.partial(mix_kernel, part),
        out_shape=jax.ShapeDtypeStruct((4, 128, 512), jnp.float32),
        in_specs=[SMEM] + [pl.BlockSpec(memory_space=pl.ANY)] * 5 + [VMEM],
        out_specs=VMEM,
        scratch_shapes=[
            pltpu.VMEM((256, 1024), jnp.bfloat16),
            pltpu.SemaphoreType.DMA((4,)),
        ],
        compiler_params=pltpu.CompilerParams(vmem_limit_bytes=8 * 1024 * 1024),
        cost_estimate=pl.CostEstimate(flops=600_000_000, bytes_accessed=4_000_000, transcendentals=0),
        name=("keep", "send")[part],
    )(table, *operands)


def body(features, short_filter, decay_rate, residue, skip, out_weight, axes, first, carry, back, mix):
    index = lax.axis_index(axes)
    yl, x, core = index % 4, index // 4 % 4, index // 16 % 2

    tie = lax.optimization_barrier
    def place(yh, z, core, x, yl):
        return yh, z // 4 * 4 + core * 2 + x // 2, x % 2, z % 4, yl

    def along(axis, by):
        def target(yh, z, core, x, yl):
            if axis == "z":
                return yh, (z + by) % 8, core, x, yl
            if axis == "x":
                return yh, z, core, (x + by) % 4, yl
            return yh, z, core, x, (yl + by) % 4

        return target

    def mine(yh, z, core, x, yl):
        return x % 2 == core

    def others(yh, z, core, x, yl):
        return x % 2 != core

    def other_core(value, sends=lambda *place: True):
        return move(value, axes, lambda yh, z, core, x, yl: (yh, z, 1 - core, x, yl), sends)

    along_z = [[(yh * 8 + z) * 2 + core for z in range(8)] for yh in range(2) for core in range(2)]

    feat = features.transpose(1, 0, 2)
    ends, query, drive, half, own = first(feat, short_filter, decay_rate)
    ends = lax.all_to_all(ends, "ctx", 0, 0, tiled=True)
    ctx = index // 16
    rate = lax.dynamic_slice(decay_rate, (ctx // 4 * 2, ctx % 4 * 128), (2, 128))
    gain = residue * jnp.sqrt(-jnp.expm1(-2.0 * decay_rate))
    ends, rate, gain, out_weight = tie((ends, rate, gain, out_weight))
    weight = move(out_weight, axes, place)
    carried = carry(ends, rate)
    incoming = lax.all_to_all(carried, "ctx", 0, 0, tiled=True).reshape(256, 128)
    incoming, weight = tie((incoming, weight))
    weights = lax.all_gather(weight, "ctx", axis_index_groups=along_z)

    gated = back(query, drive, half, own, incoming, decay_rate, gain, skip[None])

    both = jnp.concatenate([gated, other_core(gated, others)], axis=0)
    beyond = move(both, axes, lambda yh, z, core, x, yl: (1 - yh, z, core, x, yl), mine)
    line = jnp.concatenate([both, beyond], axis=0)
    fwd = move(line, axes, along("x", 1), mine)
    bwd = move(line, axes, along("x", -1), mine)
    half_rows = line.shape[0] // 2
    hf = move(fwd[:half_rows], axes, along("x", 1), others)
    hb = move(bwd[half_rows:], axes, along("x", -1), others)

    matched = x % 2 == core
    low = jnp.where(matched, x // 2, (x + 3) % 4 // 2)
    high = jnp.where(matched, 1 - x // 2, (x + 1) % 4 // 2)
    table = jnp.stack([matched.astype(jnp.int32), yl, low, high, x]).astype(jnp.int32)
    operands = (table, line, fwd, bwd, hf, hb, weights.reshape(4, 1024, 256))
    sent = other_core(mix(1, *operands))
    keep = mix(0, *operands)

    blocks = keep + sent
    parts = [move(blocks[d].astype(jnp.bfloat16), axes, along("yl", d)) for d in range(1, 4)]
    total = blocks[0] + sum(part.astype(jnp.float32) for part in parts)

    def home(yh, z, core, x, yl):
        block = yl ^ x
        return yh ^ (block // 2), z, core, yh * 2 + block % 2, x

    return move(total.astype(jnp.bfloat16), axes, home)


def shards(*arguments):
    return body(*arguments, AXES, first, carry, back, mix)


def solution(mesh):
    in_specs = (
        P("ctx", None, "tp"),
        P(None, None, "tp"),
        P(None, "tp"),
        P(None, "tp"),
        P("tp"),
        P("tp", "ctx"),
    )
    return jax.shard_map(shards, mesh=mesh, in_specs=in_specs, out_specs=P("ctx", "tp"), check_vma=False)
```
